32 devices in a mesh: dp: 8 (over z, core), clus: 4 (over y, x).
Axes of the slice: x: 2, y: 2, z: 4, core: 2. Of those that a mesh axis runs over, the one named last changes fastest.
Arguments:
- rows: bfloat16 [8192, 1024], P(('dp', 'clus')), may hold values from -8 to 8
- fine_assign: int32 [8192], P(('dp', 'clus')), may hold values from 0 to 8191, as said below
- parent1: int32 [8192], P(('dp', 'clus')), may hold values from 0 to 2047, as said below
- parent2: int32 [2048], P('dp'), may hold values from 0 to 511
- parent3: int32 [512], replicated, may hold values from 0 to 63
- shrink: float32 [4], replicated, may hold values from 0.5 to 2
Outputs:
- fine_centroids: bfloat16 [8192, 1024], P(('dp', 'clus'))
- mid_centroids: bfloat16 [2048, 1024], P(('dp', 'clus'))
- coarse_centroids: bfloat16 [512, 1024], P(('dp', 'clus'))
- spread: float32 [8192], P(('dp', 'clus'))
The draws below stay inside these ranges and needn't reach their ends.
Inputs may be any that keep to these rules, and one draw needn't show every extreme that they name: `fine_assign`: devices are numbered d = dp index * 4 + clus index, and fine centroid k is owned by device k // 256. Every row of device d names a fine centroid owned by a device of the same dp index. At most 128 rows of one device name centroids of one owner, and in every dp group some owner is named by exactly 128 rows of each device of the group. parent1[k] is one of the 256 second-level centroids g * 256 to g * 256 + 255, with g = k // 1024.
All inputs are finite; a program needn't handle non-finite values.
Results may differ from the reference program's by a relative error of at most 0.0035.
Values may be sent and summed in bfloat16 or wider, within the bound.
A program may use at most 64 MiB of HBM per device.

```python
import math
import jax
import jax.numpy as jnp

D = 1024
ROWS_DEV = 256
F1 = 256
F2 = 256
K3 = 512
K4 = 64
ROWS = 8192
K1 = 8192
K2 = 2048
N_DP = 8
N_CLUS = 4
DEVICES = 32


def make_parent1(key):
    index = jnp.arange(F1 * DEVICES, dtype=jnp.int32)
    group = index // (F1 * N_CLUS)
    pick = jax.random.randint(jax.random.fold_in(key, 11), (F1 * DEVICES,), 0, F2)
    return (group * F2 + pick).astype(jnp.int32)


def make_parent2(key):
    return jax.random.randint(jax.random.fold_in(key, 12), (F2 * N_DP,), 0, K3).astype(jnp.int32)


def make_parent3(key):
    return jax.random.randint(jax.random.fold_in(key, 13), (K3,), 0, K4).astype(jnp.int32)


def make_assign(key):
    base = jax.random.fold_in(key, 14)
    key_full, key_position, key_order, key_local = jax.random.split(base, 4)
    capacity_limit = 2 * ROWS_DEV // N_CLUS
    position_count = N_CLUS * capacity_limit
    full_row = jax.random.randint(key_full, (N_DP,), 0, N_CLUS)
    complete_per_shard = jnp.repeat(full_row, N_CLUS)
    position_index = jnp.arange(position_count, dtype=jnp.int32)
    random_jitter = jax.random.randint(key_position, (DEVICES, position_count), 0, 2 ** 14)
    extra_reward = jnp.where(position_index[None, :] // capacity_limit == complete_per_shard[:, None], 2 ** 28, 0)
    rating_value = random_jitter * position_count + position_index[None, :] + extra_reward
    chosen = jnp.argsort(-rating_value, axis=1)[:, :ROWS_DEV]
    target = (chosen // capacity_limit).astype(jnp.int32)
    mixing = jax.random.randint(key_order, (DEVICES, ROWS_DEV), 0, 2 ** 14) * ROWS_DEV + jnp.arange(ROWS_DEV)[None, :]
    order = jnp.argsort(mixing, axis=1)
    target = jnp.take_along_axis(target, order, axis=1)
    local = jax.random.randint(key_local, (DEVICES, ROWS_DEV), 0, F1)
    dev_dp = (jnp.arange(DEVICES, dtype=jnp.int32) // N_CLUS)[:, None]
    fine = (dev_dp * N_CLUS + target) * F1 + local
    return fine.reshape(-1).astype(jnp.int32)


def offsets(key, labels):
    return jax.vmap(lambda label: jax.random.normal(jax.random.fold_in(key, label), (D,), jnp.float32))(labels)


def draw_fine_assign(key, part):
    return make_assign(key)


def draw_parent1(key, part):
    return make_parent1(key)


def draw_parent2(key, part):
    return make_parent2(key)


def draw_parent3(key, part):
    return make_parent3(key)


def draw_rows(key, part):
    first = make_assign(key)
    second = make_parent1(key)[first]
    third = make_parent2(key)[second]
    fourth = make_parent3(key)[third]
    values = offsets(jax.random.fold_in(key, 21), fourth)
    values = values + 0.8 * offsets(jax.random.fold_in(key, 22), third)
    values = values + 0.6 * offsets(jax.random.fold_in(key, 23), second)
    values = values + 0.5 * offsets(jax.random.fold_in(key, 24), first)
    values = values + 0.5 * jax.random.normal(jax.random.fold_in(key, 25), (ROWS_DEV * DEVICES, D), jnp.float32)
    return jnp.clip(values, -8.0, 8.0).astype(jnp.bfloat16)


def setup_inputs(seed: int = 0) -> dict:
    key_of = jax.random.split(jax.random.key(seed), 7)
    rows = draw_rows(jax.random.fold_in(key_of[6], 71), 0)
    fine_assign = draw_fine_assign(jax.random.fold_in(key_of[6], 71), 0)
    parent1 = draw_parent1(jax.random.fold_in(key_of[6], 71), 0)
    parent2 = draw_parent2(jax.random.fold_in(key_of[6], 71), 0)
    parent3 = draw_parent3(jax.random.fold_in(key_of[6], 71), 0)
    shrink = jnp.clip(jnp.exp(jax.random.uniform(key_of[5], (4,), jnp.float32, math.log(0.5), math.log(2.0))), 0.5, 2.0)
    return dict(rows=rows, fine_assign=fine_assign, parent1=parent1, parent2=parent2, parent3=parent3, shrink=shrink)


def shrunk(sums, counts, prior, weight):
    return (sums + weight * prior) / (counts + weight)[:, None]


def reference(rows, fine_assign, parent1, parent2, parent3, shrink):
    ones = jnp.ones(fine_assign.shape, jnp.float32)
    fine_sums = jax.ops.segment_sum(rows.astype(jnp.float32), fine_assign, num_segments=K1)
    fine_counts = jax.ops.segment_sum(ones, fine_assign, num_segments=K1)
    middle_sums = jax.ops.segment_sum(fine_sums, parent1, num_segments=K2)
    middle_counts = jax.ops.segment_sum(fine_counts, parent1, num_segments=K2)
    third_sums = jax.ops.segment_sum(middle_sums, parent2, num_segments=K3)
    third_counts = jax.ops.segment_sum(middle_counts, parent2, num_segments=K3)
    top_sums = jax.ops.segment_sum(third_sums, parent3, num_segments=K4)
    top_counts = jax.ops.segment_sum(third_counts, parent3, num_segments=K4)
    center = jnp.sum(top_sums, axis=0) / ROWS
    top_means = shrunk(top_sums, top_counts, center[None, :], shrink[0] * (ROWS / K4))
    third_means = shrunk(third_sums, third_counts, top_means[parent3], shrink[1] * (ROWS / K3))
    middle_means = shrunk(middle_sums, middle_counts, third_means[parent2], shrink[2] * (ROWS / K2))
    fine_means = shrunk(fine_sums, fine_counts, middle_means[parent1], shrink[3] * (ROWS / K1))
    fine_out = fine_means.astype(jnp.bfloat16)
    diff = rows.astype(jnp.float32) - fine_out.astype(jnp.float32)[fine_assign]
    error = jnp.sum(diff * diff, axis=1)
    spread = jax.ops.segment_sum(error, fine_assign, num_segments=K1) / (D * (fine_counts + 1.0))
    return fine_out, middle_means.astype(jnp.bfloat16), third_means.astype(jnp.bfloat16), spread
```

```python
import functools

import jax
import jax.numpy as jnp
from jax import lax
from jax.experimental import pallas as pl
from jax.experimental.pallas import tpu as pltpu
from jax.sharding import PartitionSpec as P

K4 = 64


HIGH = lax.Precision.HIGHEST


def shrunk(sums, counts, prior, weight):
    return (sums + weight * prior) / (counts + weight)[:, None]


def local(rows, fine_assign, parent1, parent2, parent3, shrink):
    groups = lax.axis_size("clus")
    dp_count = lax.axis_size("dp")
    devices = groups * dp_count
    clus_index = lax.axis_index("clus")
    dp_index = lax.axis_index("dp")
    count = rows.shape[0]
    width = rows.shape[1]
    fine_dev = parent1.shape[0]
    middle_dp = parent2.shape[0]
    third = parent3.shape[0]
    slots = 2 * count // groups
    total = count * devices
    weight_top = shrink[0] * (total / K4)
    weight_third = shrink[1] * (total / third)
    weight_middle = shrink[2] * (total / (middle_dp * dp_count))
    weight_fine = shrink[3] * (total / (fine_dev * devices))
    local_ids = fine_assign - dp_index * groups * fine_dev
    target = local_ids // fine_dev
    within = local_ids - target * fine_dev
    target_hot = (target[:, None] == jnp.arange(groups)[None, :]).astype(jnp.bfloat16)
    earlier = (jnp.arange(count)[:, None] > jnp.arange(count)[None, :]).astype(jnp.bfloat16)
    before = jnp.dot(earlier, target_hot, preferred_element_type=jnp.float32)
    rank = jnp.sum(before * target_hot.astype(jnp.float32), axis=1).astype(jnp.int32)
    slot_of = target * slots + rank
    source = (
        jnp.full((groups * slots,), count, jnp.int32)
        .at[slot_of]
        .set(jnp.arange(count, dtype=jnp.int32))
    )
    padded = jnp.concatenate([rows, jnp.zeros((1, width), jnp.bfloat16)], axis=0)
    send_rows = padded[source].reshape(groups, slots, width)
    send_ids = jnp.concatenate([within, jnp.full((1,), -1, jnp.int32)])[source].reshape(
        groups, slots
    )
    got_rows, got_ids = (
        lax.all_to_all(send_rows, "clus", split_axis=0, concat_axis=0, tiled=True),
        lax.all_to_all(send_ids, "clus", split_axis=0, concat_axis=0, tiled=True),
    )
    got_rows = got_rows.reshape(groups * slots, width)
    got_ids = got_ids.reshape(groups * slots)
    member = (got_ids[:, None] == jnp.arange(fine_dev)[None, :]).astype(jnp.bfloat16)
    contract = (((0,), (0,)), ((), ()))
    fine_sums = lax.dot_general(member, got_rows, contract, preferred_element_type=jnp.float32)
    fine_counts = jnp.sum(member.astype(jnp.float32), axis=0)
    middle_local = parent1 - dp_index * middle_dp
    child_hot = (jnp.arange(middle_dp)[:, None] == middle_local[None, :]).astype(jnp.float32)
    middle_part = jnp.dot(child_hot, fine_sums, precision=HIGH)
    middle_tally = jnp.dot(child_hot, fine_counts, precision=HIGH)
    share = middle_dp // groups
    offset = clus_index * share
    middle_sums, middle_counts = (
        lax.psum_scatter(middle_part, "clus", scatter_dimension=0, tiled=True),
        lax.psum_scatter(middle_tally, "clus", scatter_dimension=0, tiled=True),
    )
    own_parent2 = lax.dynamic_slice_in_dim(parent2, offset, share, 0)
    third_share = third // devices
    third_start = (dp_index * groups + clus_index) * third_share
    third_hot = (jnp.arange(third)[:, None] == own_parent2[None, :]).astype(jnp.float32)
    third_part = jnp.dot(third_hot, middle_sums, precision=HIGH)
    third_tally = jnp.dot(third_hot, middle_counts, precision=HIGH)
    third_sums, third_counts = lax.psum((third_part, third_tally), ("dp", "clus"))
    top_hot = (jnp.arange(K4)[:, None] == parent3[None, :]).astype(jnp.float32)
    top_sums = jnp.dot(top_hot, third_sums, precision=HIGH)
    top_counts = jnp.dot(top_hot, third_counts, precision=HIGH)
    center = jnp.sum(top_sums, axis=0) / total
    top_means = shrunk(top_sums, top_counts, center[None, :], weight_top)
    third_means = shrunk(
        third_sums, third_counts, jnp.dot(top_hot.T, top_means, precision=HIGH), weight_third
    )
    third_out = lax.dynamic_slice_in_dim(third_means, third_start, third_share, 0)
    parent_hot = (own_parent2[:, None] == jnp.arange(third)[None, :]).astype(jnp.float32)
    middle_out = shrunk(
        middle_sums, middle_counts, jnp.dot(parent_hot, third_means, precision=HIGH), weight_middle
    )
    middle_means = lax.all_gather(middle_out, "clus", axis=0, tiled=True)
    fine_means = shrunk(
        fine_sums, fine_counts, jnp.dot(child_hot.T, middle_means, precision=HIGH), weight_fine
    )
    fine_out = fine_means.astype(jnp.bfloat16)
    back = jnp.dot(member, fine_out, preferred_element_type=jnp.float32)
    diff = got_rows.astype(jnp.float32) - back
    row_error = jnp.sum(diff * diff, axis=1)
    spread = jnp.sum(member.astype(jnp.float32) * row_error[:, None], axis=0) / (
        width * (fine_counts + 1.0)
    )
    return (fine_out, middle_out.astype(jnp.bfloat16), third_out.astype(jnp.bfloat16), spread)


LANES = 128
BF = jnp.bfloat16
F32 = jnp.float32
MESH = pl.DeviceIdType.MESH


def rows_hot(size, ids):
    shape = (size, ids.shape[1])
    return jnp.where(lax.broadcasted_iota(jnp.int32, shape, 0) == ids, 1.0, 0.0).astype(BF)


def column_of(ids):
    return jnp.broadcast_to(ids.astype(F32), (LANES, ids.shape[1])).T


def lanes_hot(column, start):
    lane = lax.broadcasted_iota(jnp.int32, column.shape, 1).astype(F32) + float(start)
    return jnp.where(column == lane, 1.0, 0.0).astype(BF)


def dot(a, b):
    return jnp.dot(a, b, preferred_element_type=F32)


def pieces(x, count):
    out = []
    for _ in range(count):
        part = x.astype(BF)
        out.append(part)
        x = x - part.astype(F32)
    return out


def dot_left(x, hot, count=3):
    return sum(dot(part, hot) for part in pieces(x, count))


def widen(column, width):
    return jnp.concatenate([column] * (width // LANES), axis=1)


def sweep(
    n,
    m,
    fa_ref,
    p1_ref,
    p2_ref,
    p3_ref,
    shrink_ref,
    rows_ref,
    fine_ref,
    mid_ref,
    coarse_ref,
    spread_ref,
    fa_all,
    p1_all,
    got,
    h1f,
    h2f,
    h3f,
    h1r,
    h1m,
    h23,
    sums1,
    sums2,
    part_own,
    part_all,
    cnt_own,
    cnt_all,
    means3,
    fine_own,
    mid_own,
    coarse_own,
    err_own,
    err_all,
    tally,
    id_send,
    id_recv,
    row_send,
    row_recv,
    part_send,
    part_recv,
    cnt_send,
    cnt_recv,
    back_send,
    back_recv,
    out_send,
    out_recv,
    local_sem,
):
    me = lax.axis_index("clus")
    dp = lax.axis_index("dp")
    count, width = rows_ref.shape
    share = width // n
    fine_dev = p1_ref.shape[1]
    middle = p2_ref.shape[1]
    third = p3_ref.shape[1]
    devices = n * m
    total = count * devices
    fine = n * fine_dev
    thin = share // m
    mid_share = middle // n
    third_share = third // devices
    w4 = shrink_ref[0] * (total / K4)
    w3 = shrink_ref[1] * (total / third)
    w2 = shrink_ref[2] * (total / (middle * m))
    w1 = shrink_ref[3] * (total / (fine_dev * devices))

    def span(index, size):
        return pl.ds(pl.multiple_of(index * size, size), size)

    def to_clus(k, src, dst, send, recv):
        return pltpu.make_async_remote_copy(
            src_ref=src,
            dst_ref=dst,
            send_sem=send,
            recv_sem=recv,
            device_id={"clus": lax.rem(me + k, n)},
            device_id_type=MESH,
        )

    def to_dp(k, src, dst, send, recv):
        return pltpu.make_async_remote_copy(
            src_ref=src,
            dst_ref=dst,
            send_sem=send,
            recv_sem=recv,
            device_id={"dp": lax.rem(dp + k, m)},
            device_id_type=MESH,
        )

    barrier = pltpu.get_barrier_semaphore()
    for k in range(1, n):
        pl.semaphore_signal(
            barrier, inc=1, device_id={"clus": lax.rem(me + k, n)}, device_id_type=MESH
        )
    for k in range(1, m):
        pl.semaphore_signal(
            barrier, inc=1, device_id={"dp": lax.rem(dp + k, m)}, device_id_type=MESH
        )
    own_rows = pltpu.make_async_copy(
        rows_ref.at[:, span(me, share)], got.at[span(me, count), :], local_sem.at[0]
    )
    own_rows.start()
    fa_all[me] = fa_ref[...]
    p1_all[me] = p1_ref[...]
    pl.semaphore_wait(barrier, n - 1 + m - 1)

    id_copies = []
    row_copies = []
    for k in range(1, n):
        id_copies.append(to_clus(k, fa_ref, fa_all.at[me], id_send.at[0, k], id_recv.at[0, k]))
        id_copies.append(to_clus(k, p1_ref, p1_all.at[me], id_send.at[1, k], id_recv.at[1, k]))
    for copy in id_copies:
        copy.start()
    for k in range(1, n):
        peer = lax.rem(me + k, n)
        copy = to_clus(
            k,
            rows_ref.at[:, span(peer, share)],
            got.at[span(me, count), :],
            row_send.at[k],
            row_recv.at[k],
        )
        copy.start()
        row_copies.append(copy)

    p2_row = p2_ref[...]
    p3_row = p3_ref[...]
    h23[...] = rows_hot(third, p2_row)
    h4 = lanes_hot(column_of(p3_row), 0)
    h4f = rows_hot(LANES, p3_row)
    high = p2_row // 256
    top_line = lax.broadcasted_iota(jnp.int32, (16, middle), 0) == 0
    p2_split = jnp.where(top_line, high, p2_row - high * 256).astype(F32).astype(BF)

    for copy in id_copies:
        copy.wait_recv()
    fa_row = jnp.concatenate([fa_all[i] for i in range(n)], axis=1) - dp * fine
    p1_row = jnp.concatenate([p1_all[i] for i in range(n)], axis=1) - dp * middle
    h1f[...] = rows_hot(fine, fa_row)
    p1_lines = jnp.broadcast_to(p1_row, (16, fine)).astype(F32).astype(BF)
    mid_row = dot(p1_lines, h1f[...])[0:1].astype(jnp.int32)
    h2f[...] = rows_hot(middle, mid_row)
    halves = dot(p2_split, h2f[...])
    third_row = (halves[0:1] * 256.0 + halves[1:2]).astype(jnp.int32)
    h3f[...] = rows_hot(third, third_row)
    ones = jnp.ones((n * count, LANES), BF)
    cnt_part = dot(h3f[...], ones).T[0:1]
    cnt_own[...] = cnt_part
    cnt_all[dp] = cnt_part
    dp_copies = []
    for k in range(1, m):
        copy = to_dp(k, cnt_own, cnt_all.at[dp], cnt_send.at[k], cnt_recv.at[k])
        copy.start()
        dp_copies.append(copy)

    own_rows.wait()
    for copy in row_copies:
        copy.wait_recv()
    part_own[...] = dot(h3f[...], got[...]).T
    for k in range(1, m):
        peer = lax.rem(dp + k, m)
        copy = to_dp(
            k, part_own.at[span(peer, thin), :], part_all.at[dp], part_send.at[k], part_recv.at[k]
        )
        copy.start()
        dp_copies.append(copy)

    sums1[...] = dot(h1f[...], got[...])
    sums2[...] = dot(h2f[...], got[...])
    scale1 = 1.0 / (dot(h1f[...], ones) + w1)
    scale2 = 1.0 / (dot(h2f[...], ones) + w2)
    fa_column = column_of(fa_row)
    for j in range(0, fine, LANES):
        h1r[:, j : j + LANES] = lanes_hot(fa_column, j)
    p1_column = column_of(p1_row)
    for j in range(0, middle, LANES):
        h1m[:, j : j + LANES] = lanes_hot(p1_column, j)
    part_all[dp] = part_own[span(dp, thin), :]

    for copy in dp_copies:
        copy.wait_recv()
    sums3 = part_all[0]
    cnt3 = cnt_all[0]
    for i in range(1, m):
        sums3 = sums3 + part_all[i]
        cnt3 = cnt3 + cnt_all[i]
    sums4 = dot_left(sums3, h4)
    cnt4 = dot_left(jnp.broadcast_to(cnt3, (16, third)), h4)[0:1]
    center = jnp.sum(sums4, axis=1, keepdims=True) / total
    means4 = (sums4 + w4 * center) / (cnt4 + w4)
    means3[dp] = ((sums3 + w3 * dot_left(means4, h4f)) / (cnt3 + w3)).astype(BF)
    back_copies = []
    for k in range(1, m):
        copy = to_dp(k, means3.at[dp], means3.at[dp], back_send.at[k], back_recv.at[k])
        copy.start()
        back_copies.append(copy)
    for copy in back_copies:
        copy.wait_recv()

    means3_all = means3[...].reshape(share, third)
    prior2 = dot(means3_all, h23[...]).T
    means2 = (sums2[...] + w2 * prior2) * widen(scale2, share)
    prior1 = sum(dot(h1m[...], part) for part in pieces(means2, 2))
    fine_own[...] = ((sums1[...] + w1 * prior1) * widen(scale1, share)).astype(BF)
    mid_own[...] = means2.astype(BF)
    coarse_own[...] = means3_all.astype(F32).T.astype(BF)
    columns = span(me, share)
    out_copies = []
    local_copies = []
    plan = (
        (fine_own, fine_ref, lambda peer: span(peer, fine_dev)),
        (mid_own, mid_ref, lambda peer: span(peer, mid_share)),
        (coarse_own, coarse_ref, lambda peer: span(dp * n + peer, third_share)),
    )
    for which, (src, dst, place) in enumerate(plan):
        for k in range(1, n):
            peer = lax.rem(me + k, n)
            copy = to_clus(
                k,
                src.at[place(peer), :],
                dst.at[:, columns],
                out_send.at[which, k],
                out_recv.at[which, k],
            )
            copy.start()
            out_copies.append(copy)
        copy = pltpu.make_async_copy(
            src.at[place(me), :], dst.at[:, columns], local_sem.at[1 + which]
        )
        copy.start()
        local_copies.append(copy)

    diff = got[...].astype(F32) - dot(h1r[...], fine_own[...])
    square = diff * diff
    folded = square[:, :LANES]
    for j in range(LANES, share, LANES):
        folded = folded + square[:, j : j + LANES]
    err_row = jnp.sum(folded.T, axis=0, keepdims=True)
    parts = pieces(err_row, 3)
    line = lax.broadcasted_iota(jnp.int32, (16, n * count), 0)
    stack = jnp.where(line == 3, 1.0, 0.0)
    for i, part in enumerate(parts):
        stack = jnp.where(line == i, part.astype(F32), stack)
    by_fine = dot(stack.astype(BF), h1r[...])
    err_fine = by_fine[0:1] + by_fine[1:2] + by_fine[2:3]
    for i in range(n):
        err_own[i] = err_fine[:, i * fine_dev : (i + 1) * fine_dev]
        tally[i] = by_fine[3:4, i * fine_dev : (i + 1) * fine_dev]
    err_copies = []
    for k in range(1, n):
        peer = lax.rem(me + k, n)
        copy = to_clus(k, err_own.at[peer], err_all.at[me], out_send.at[3, k], out_recv.at[3, k])
        copy.start()
        err_copies.append(copy)
    err_all[me] = err_own[me]
    for copy in err_copies:
        copy.wait_recv()
    err = err_all[0]
    for i in range(1, n):
        err = err + err_all[i]
    spread_ref[...] = err / (width * (tally[me] + 1.0))
    for copy in local_copies:
        copy.wait()
    for copy in out_copies:
        copy.wait_recv()
    for copy in id_copies + row_copies + dp_copies + back_copies + out_copies + err_copies:
        copy.wait_send()


def fused(rows, fine_assign, parent1, parent2, parent3, shrink):
    n = lax.axis_size("clus")
    m = lax.axis_size("dp")
    count, width = rows.shape
    fine_dev = parent1.shape[0]
    middle = parent2.shape[0]
    third = parent3.shape[0]
    share = width // n
    thin = share // m
    fine = n * fine_dev
    total_rows = n * count
    vmem = pl.BlockSpec(memory_space=pltpu.VMEM)
    dma = pltpu.SemaphoreType.DMA
    fine_out, mid_out, coarse_out, spread = pl.pallas_call(
        functools.partial(sweep, n, m),
        out_shape=(
            jax.ShapeDtypeStruct((fine_dev, width), BF),
            jax.ShapeDtypeStruct((middle // n, width), BF),
            jax.ShapeDtypeStruct((third // (n * m), width), BF),
            jax.ShapeDtypeStruct((1, fine_dev), F32),
        ),
        in_specs=[vmem] * 4
        + [pl.BlockSpec(memory_space=pltpu.SMEM), pl.BlockSpec(memory_space=pl.ANY)],
        out_specs=[vmem] * 4,
        scratch_shapes=[
            pltpu.VMEM((n, 1, count), jnp.int32),
            pltpu.VMEM((n, 1, fine_dev), jnp.int32),
            pltpu.VMEM((total_rows, share), BF),
            pltpu.VMEM((fine, total_rows), BF),
            pltpu.VMEM((middle, total_rows), BF),
            pltpu.VMEM((third, total_rows), BF),
            pltpu.VMEM((total_rows, fine), BF),
            pltpu.VMEM((fine, middle), BF),
            pltpu.VMEM((third, middle), BF),
            pltpu.VMEM((fine, share), F32),
            pltpu.VMEM((middle, share), F32),
            pltpu.VMEM((share, third), F32),
            pltpu.VMEM((m, thin, third), F32),
            pltpu.VMEM((1, third), F32),
            pltpu.VMEM((m, 1, third), F32),
            pltpu.VMEM((m, thin, third), BF),
            pltpu.VMEM((fine, share), BF),
            pltpu.VMEM((middle, share), BF),
            pltpu.VMEM((third, share), BF),
            pltpu.VMEM((n, 1, fine_dev), F32),
            pltpu.VMEM((n, 1, fine_dev), F32),
            pltpu.VMEM((n, 1, fine_dev), F32),
            dma((2, n)),
            dma((2, n)),
            dma((n,)),
            dma((n,)),
            dma((m,)),
            dma((m,)),
            dma((m,)),
            dma((m,)),
            dma((m,)),
            dma((m,)),
            dma((4, n)),
            dma((4, n)),
            dma((4,)),
        ],
        compiler_params=pltpu.CompilerParams(
            collective_id=0, has_side_effects=True, vmem_limit_bytes=60 << 20
        ),
        name="sweep",
    )(
        fine_assign.reshape(1, count),
        parent1.reshape(1, fine_dev),
        parent2.reshape(1, middle),
        parent3.reshape(1, third),
        shrink,
        rows,
    )
    return fine_out, mid_out, coarse_out, spread.reshape(fine_dev)


def fits(rows, fine_assign, parent1, parent2, parent3):
    n = lax.axis_size("clus")
    m = lax.axis_size("dp")
    return (
        rows.shape[1] % (n * LANES) == 0
        and (rows.shape[1] // n) % (m * 16) == 0
        and rows.shape[0] % LANES == 0
        and parent1.shape[0] % LANES == 0
        and parent2.shape[0] % LANES == 0
        and parent2.shape[0] <= 256
        and parent2.shape[0] % (n * 16) == 0
        and parent3.shape[0] % LANES == 0
        and parent3.shape[0] % (n * m * 16) == 0
    )


def step(rows, fine_assign, parent1, parent2, parent3, shrink):
    form = fused if fits(rows, fine_assign, parent1, parent2, parent3) else local
    return form(rows, fine_assign, parent1, parent2, parent3, shrink)


def solution(mesh):
    placed = (P(("dp", "clus"), None), P(("dp", "clus")), P(("dp", "clus")), P("dp"), P(), P())
    return jax.shard_map(
        step,
        mesh=mesh,
        in_specs=placed,
        out_specs=(
            P(("dp", "clus"), None),
            P(("dp", "clus"), None),
            P(("dp", "clus"), None),
            P(("dp", "clus")),
        ),
        check_vma=False,
    )
```

```python
import functools

import jax
import jax.numpy as jnp
from jax import lax
from jax.experimental import pallas as pl
from jax.experimental.pallas import tpu as pltpu
from jax.sharding import PartitionSpec as P

K4 = 64


HIGH = lax.Precision.HIGHEST


def shrunk(sums, counts, prior, weight):
    return (sums + weight * prior) / (counts + weight)[:, None]


def local(rows, fine_assign, parent1, parent2, parent3, shrink):
    groups = lax.axis_size("clus")
    dp_count = lax.axis_size("dp")
    devices = groups * dp_count
    clus_index = lax.axis_index("clus")
    dp_index = lax.axis_index("dp")
    count = rows.shape[0]
    width = rows.shape[1]
    fine_dev = parent1.shape[0]
    middle_dp = parent2.shape[0]
    third = parent3.shape[0]
    slots = 2 * count // groups
    total = count * devices
    weight_top = shrink[0] * (total / K4)
    weight_third = shrink[1] * (total / third)
    weight_middle = shrink[2] * (total / (middle_dp * dp_count))
    weight_fine = shrink[3] * (total / (fine_dev * devices))
    local_ids = fine_assign - dp_index * groups * fine_dev
    target = local_ids // fine_dev
    within = local_ids - target * fine_dev
    target_hot = (target[:, None] == jnp.arange(groups)[None, :]).astype(jnp.bfloat16)
    earlier = (jnp.arange(count)[:, None] > jnp.arange(count)[None, :]).astype(jnp.bfloat16)
    before = jnp.dot(earlier, target_hot, preferred_element_type=jnp.float32)
    rank = jnp.sum(before * target_hot.astype(jnp.float32), axis=1).astype(jnp.int32)
    slot_of = target * slots + rank
    source = (
        jnp.full((groups * slots,), count, jnp.int32)
        .at[slot_of]
        .set(jnp.arange(count, dtype=jnp.int32))
    )
    padded = jnp.concatenate([rows, jnp.zeros((1, width), jnp.bfloat16)], axis=0)
    send_rows = padded[source].reshape(groups, slots, width)
    send_ids = jnp.concatenate([within, jnp.full((1,), -1, jnp.int32)])[source].reshape(
        groups, slots
    )
    got_rows, got_ids = (
        lax.all_to_all(send_rows, "clus", split_axis=0, concat_axis=0, tiled=True),
        lax.all_to_all(send_ids, "clus", split_axis=0, concat_axis=0, tiled=True),
    )
    got_rows = got_rows.reshape(groups * slots, width)
    got_ids = got_ids.reshape(groups * slots)
    member = (got_ids[:, None] == jnp.arange(fine_dev)[None, :]).astype(jnp.bfloat16)
    contract = (((0,), (0,)), ((), ()))
    fine_sums = lax.dot_general(member, got_rows, contract, preferred_element_type=jnp.float32)
    fine_counts = jnp.sum(member.astype(jnp.float32), axis=0)
    middle_local = parent1 - dp_index * middle_dp
    child_hot = (jnp.arange(middle_dp)[:, None] == middle_local[None, :]).astype(jnp.float32)
    middle_part = jnp.dot(child_hot, fine_sums, precision=HIGH)
    middle_tally = jnp.dot(child_hot, fine_counts, precision=HIGH)
    share = middle_dp // groups
    offset = clus_index * share
    middle_sums, middle_counts = (
        lax.psum_scatter(middle_part, "clus", scatter_dimension=0, tiled=True),
        lax.psum_scatter(middle_tally, "clus", scatter_dimension=0, tiled=True),
    )
    own_parent2 = lax.dynamic_slice_in_dim(parent2, offset, share, 0)
    third_share = third // devices
    third_start = (dp_index * groups + clus_index) * third_share
    third_hot = (jnp.arange(third)[:, None] == own_parent2[None, :]).astype(jnp.float32)
    third_part = jnp.dot(third_hot, middle_sums, precision=HIGH)
    third_tally = jnp.dot(third_hot, middle_counts, precision=HIGH)
    third_sums, third_counts = lax.psum((third_part, third_tally), ("dp", "clus"))
    top_hot = (jnp.arange(K4)[:, None] == parent3[None, :]).astype(jnp.float32)
    top_sums = jnp.dot(top_hot, third_sums, precision=HIGH)
    top_counts = jnp.dot(top_hot, third_counts, precision=HIGH)
    center = jnp.sum(top_sums, axis=0) / total
    top_means = shrunk(top_sums, top_counts, center[None, :], weight_top)
    third_means = shrunk(
        third_sums, third_counts, jnp.dot(top_hot.T, top_means, precision=HIGH), weight_third
    )
    third_out = lax.dynamic_slice_in_dim(third_means, third_start, third_share, 0)
    parent_hot = (own_parent2[:, None] == jnp.arange(third)[None, :]).astype(jnp.float32)
    middle_out = shrunk(
        middle_sums, middle_counts, jnp.dot(parent_hot, third_means, precision=HIGH), weight_middle
    )
    middle_means = lax.all_gather(middle_out, "clus", axis=0, tiled=True)
    fine_means = shrunk(
        fine_sums, fine_counts, jnp.dot(child_hot.T, middle_means, precision=HIGH), weight_fine
    )
    fine_out = fine_means.astype(jnp.bfloat16)
    back = jnp.dot(member, fine_out, preferred_element_type=jnp.float32)
    diff = got_rows.astype(jnp.float32) - back
    row_error = jnp.sum(diff * diff, axis=1)
    spread = jnp.sum(member.astype(jnp.float32) * row_error[:, None], axis=0) / (
        width * (fine_counts + 1.0)
    )
    return (fine_out, middle_out.astype(jnp.bfloat16), third_out.astype(jnp.bfloat16), spread)


LANES = 128
BF = jnp.bfloat16
F32 = jnp.float32
MESH = pl.DeviceIdType.MESH


def rows_hot(size, ids):
    shape = (size, ids.shape[1])
    return jnp.where(lax.broadcasted_iota(jnp.int32, shape, 0) == ids, 1.0, 0.0).astype(BF)


def column_of(ids):
    return jnp.broadcast_to(ids.astype(F32), (LANES, ids.shape[1])).T


def lanes_hot(column, start):
    lane = lax.broadcasted_iota(jnp.int32, column.shape, 1).astype(F32) + float(start)
    return jnp.where(column == lane, 1.0, 0.0).astype(BF)


def dot(a, b):
    return jnp.dot(a, b, preferred_element_type=F32)


def pieces(x, count):
    out = []
    for _ in range(count):
        part = x.astype(BF)
        out.append(part)
        x = x - part.astype(F32)
    return out


def dot_left(x, hot, count=3):
    return sum(dot(part, hot) for part in pieces(x, count))


def sweep(
    n,
    m,
    fa_ref,
    p1_ref,
    p2_ref,
    p3_ref,
    shrink_ref,
    rows_ref,
    fine_ref,
    mid_ref,
    coarse_ref,
    spread_ref,
    fa_all,
    p1_all,
    got,
    h1f,
    h2f,
    h3f,
    h1r,
    h1m,
    h23,
    base1,
    base2,
    pull1,
    pull2,
    part_own,
    pair_got,
    pair_sum,
    part_all,
    cnt_own,
    cnt_all,
    means3,
    fine_own,
    mid_own,
    coarse_own,
    err_own,
    err_all,
    tally,
    id_send,
    id_recv,
    row_send,
    row_recv,
    pair_send,
    pair_recv,
    part_send,
    part_recv,
    cnt_send,
    cnt_recv,
    back_send,
    back_recv,
    relay_send,
    relay_recv,
    fine_send,
    fine_recv,
    out_send,
    out_recv,
    local_sem,
):
    me = lax.axis_index("clus")
    dp = lax.axis_index("dp")
    count, width = rows_ref.shape
    share = width // n
    chunks = share // LANES
    fine_dev = p1_ref.shape[1]
    middle = p2_ref.shape[1]
    third = p3_ref.shape[1]
    devices = n * m
    total = count * devices
    fine = n * fine_dev
    pairs = m // 2
    half = LANES // 2
    thin = half // pairs
    pair = dp // 2
    side = lax.rem(dp, 2)
    mid_share = middle // n
    third_share = third // devices
    w4 = shrink_ref[0] * (total / K4)
    w3 = shrink_ref[1] * (total / third)
    w2 = shrink_ref[2] * (total / (middle * m))
    w1 = shrink_ref[3] * (total / (fine_dev * devices))

    def span(index, size):
        return pl.ds(pl.multiple_of(index * size, size), size)

    def chunk_of(h):
        return slice(h * LANES, (h + 1) * LANES)

    def remote(src, dst, send, recv, device):
        return pltpu.make_async_remote_copy(
            src_ref=src,
            dst_ref=dst,
            send_sem=send,
            recv_sem=recv,
            device_id=device,
            device_id_type=MESH,
        )

    def clus_peer(k):
        return {"clus": lax.rem(me + k, n)}

    def dp_peer(k):
        return {"dp": lax.rem(dp + k, m)}

    def pair_peer(k):
        return {"dp": lax.rem(pair + k, pairs) * 2 + side}

    other = {"dp": pair * 2 + 1 - side}

    started = []

    def start(copies):
        for copy in copies:
            copy.start()
        started.extend(copies)
        return copies

    def arrive(copies):
        for copy in copies:
            copy.wait_recv()

    barrier = pltpu.get_barrier_semaphore()
    for k in range(1, n):
        pl.semaphore_signal(barrier, inc=1, device_id=clus_peer(k), device_id_type=MESH)
    for k in range(1, m):
        pl.semaphore_signal(barrier, inc=1, device_id=dp_peer(k), device_id_type=MESH)
    own_rows = pltpu.make_async_copy(
        rows_ref.at[:, span(me, share)], got.at[span(me, count), :], local_sem.at[0]
    )
    own_rows.start()
    fa_all[me] = fa_ref[...]
    p1_all[me] = p1_ref[...]
    p2_row = p2_ref[...]
    p3_row = p3_ref[...]
    pl.semaphore_wait(barrier, n - 1 + m - 1)

    id_copies = []
    for k in range(1, n):
        for which, (src, dst) in enumerate(((fa_ref, fa_all), (p1_ref, p1_all))):
            id_copies.append(
                remote(src, dst.at[me], id_send.at[which, k], id_recv.at[which, k], clus_peer(k))
            )
    start(id_copies)
    row_copies = []
    for h in range(chunks):
        copies = []
        for k in range(1, n):
            column = lax.rem(me + k, n) * share + h * LANES
            copies.append(
                remote(
                    rows_ref.at[:, pl.ds(pl.multiple_of(column, LANES), LANES)],
                    got.at[span(me, count), chunk_of(h)],
                    row_send.at[h, k],
                    row_recv.at[h, k],
                    clus_peer(k),
                )
            )
        row_copies.append(start(copies))

    h23[...] = rows_hot(third, p2_row)
    h4 = lanes_hot(column_of(p3_row), 0)
    h4f = rows_hot(LANES, p3_row)
    high = p2_row // 256
    top_line = lax.broadcasted_iota(jnp.int32, (16, middle), 0) == 0
    p2_split = jnp.where(top_line, high, p2_row - high * 256).astype(F32).astype(BF)

    arrive(id_copies)
    fa_row = jnp.concatenate([fa_all[i] for i in range(n)], axis=1) - dp * fine
    p1_row = jnp.concatenate([p1_all[i] for i in range(n)], axis=1) - dp * middle
    h1f[...] = rows_hot(fine, fa_row)
    p1_lines = jnp.broadcast_to(p1_row, (16, fine)).astype(F32).astype(BF)
    mid_row = dot(p1_lines, h1f[...])[0:1].astype(jnp.int32)
    h2f[...] = rows_hot(middle, mid_row)
    halves = dot(p2_split, h2f[...])
    third_row = (halves[0:1] * 256.0 + halves[1:2]).astype(jnp.int32)
    h3f[...] = rows_hot(third, third_row)
    ones = jnp.ones((n * count, LANES), BF)
    own_rows.wait()

    pair_copies = []
    part_copies = []
    back_copies = []
    relay_copies = []
    cnt_copies = []

    def sum_part(h):
        arrive(row_copies[h])
        part_own[h] = dot(h3f[...], got[:, chunk_of(h)]).T
        away = part_own.at[h, span(1 - side, half), :]
        copy = remote(away, pair_got.at[h], pair_send.at[h], pair_recv.at[h], other)
        pair_copies.append(start([copy]))

    def sum_pair(h):
        arrive(pair_copies[h])
        pair_sum[h] = part_own[h, span(side, half), :] + pair_got[h]
        copies = []
        for k in range(1, pairs):
            copies.append(
                remote(
                    pair_sum.at[h, span(lax.rem(pair + k, pairs), thin), :],
                    part_all.at[h, pair],
                    part_send.at[h, k],
                    part_recv.at[h, k],
                    pair_peer(k),
                )
            )
        part_copies.append(start(copies))
        part_all[h, pair] = pair_sum[h, span(pair, thin), :]

    def third_level(h, cnt3, cnt4):
        arrive(part_copies[h])
        sums3 = part_all[h, 0]
        for i in range(1, pairs):
            sums3 = sums3 + part_all[h, i]
        sums4 = dot_left(sums3, h4)
        center = jnp.sum(sums4, axis=1, keepdims=True) / total
        means4 = (sums4 + w4 * center) / (cnt4 + w4)
        place = span(side * pairs + pair, thin)
        means3[h, place, :] = ((sums3 + w3 * dot_left(means4, h4f)) / (cnt3 + w3)).astype(BF)
        copies = []
        for k in range(1, pairs):
            block = means3.at[h, place, :]
            copies.append(remote(block, block, back_send.at[h, k], back_recv.at[h, k], pair_peer(k)))
        back_copies.append(start(copies))

    def relay(h):
        arrive(back_copies[h])
        block = means3.at[h, span(side, half), :]
        copy = remote(block, block, relay_send.at[h], relay_recv.at[h], other)
        relay_copies.append(start([copy]))

    sum_part(0)
    cnt_part = dot(h3f[...], ones).T[0:1]
    cnt_own[...] = cnt_part
    cnt_all[dp] = cnt_part
    for k in range(1, m):
        cnt_copies.append(
            remote(cnt_own, cnt_all.at[dp], cnt_send.at[k], cnt_recv.at[k], dp_peer(k))
        )
    start(cnt_copies)
    p1_column = column_of(p1_row)
    for j in range(0, middle, LANES):
        h1m[:, j : j + LANES] = lanes_hot(p1_column, j)
    for h in range(1, chunks):
        sum_pair(h - 1)
        sum_part(h)
    scale1 = 1.0 / (dot(h1f[...], ones) + w1)
    scale2 = 1.0 / (dot(h2f[...], ones) + w2)
    pull1[...] = w1 * scale1
    pull2[...] = w2 * scale2
    sum_pair(chunks - 1)
    for h in range(chunks):
        base1[:, chunk_of(h)] = dot(h1f[...], got[:, chunk_of(h)]) * scale1
        base2[:, chunk_of(h)] = dot(h2f[...], got[:, chunk_of(h)]) * scale2
    arrive(cnt_copies)
    cnt3 = cnt_all[0]
    for i in range(1, m):
        cnt3 = cnt3 + cnt_all[i]
    cnt4 = dot_left(jnp.broadcast_to(cnt3, (16, third)), h4)[0:1]
    for h in range(chunks):
        third_level(h, cnt3, cnt4)
    fa_column = column_of(fa_row)
    for j in range(0, fine, LANES):
        h1r[:, j : j + LANES] = lanes_hot(fa_column, j)
    for h in range(chunks):
        relay(h)

    fine_copies = []
    local_copies = []
    for h in range(chunks):
        arrive(relay_copies[h])
        columns = pl.ds(pl.multiple_of(me * share + h * LANES, LANES), LANES)
        means2 = base2[:, chunk_of(h)] + pull2[...] * dot(means3[h], h23[...]).T
        mid_own[:, chunk_of(h)] = means2.astype(BF)
        parts = pieces(means2, 2)
        for k in (*range(1, n), 0):
            block = span(lax.rem(me + k, n), fine_dev)
            prior = sum(dot(h1m[block, :], part) for part in parts)
            means1 = base1[block, chunk_of(h)] + pull1[block, :] * prior
            fine_own[block, chunk_of(h)] = means1.astype(BF)
            src = fine_own.at[block, chunk_of(h)]
            dst = fine_ref.at[:, columns]
            if k:
                copy = remote(src, dst, fine_send.at[h, k], fine_recv.at[h, k], clus_peer(k))
                fine_copies.extend(start([copy]))
            else:
                copy = pltpu.make_async_copy(src, dst, local_sem.at[3 + h])
                copy.start()
                local_copies.append(copy)
    for h in range(chunks):
        coarse_own[:, chunk_of(h)] = means3[h].astype(F32).T.astype(BF)
    columns = span(me, share)
    out_copies = []
    plan = (
        (mid_own, mid_ref, lambda peer: span(peer, mid_share)),
        (coarse_own, coarse_ref, lambda peer: span(dp * n + peer, third_share)),
    )
    for which, (src, dst, place) in enumerate(plan):
        for k in range(1, n):
            out_copies.append(
                remote(
                    src.at[place(lax.rem(me + k, n)), :],
                    dst.at[:, columns],
                    out_send.at[which, k],
                    out_recv.at[which, k],
                    clus_peer(k),
                )
            )
        copy = pltpu.make_async_copy(
            src.at[place(me), :], dst.at[:, columns], local_sem.at[1 + which]
        )
        copy.start()
        local_copies.append(copy)
    start(out_copies)

    diff = got[...].astype(F32) - dot(h1r[...], fine_own[...])
    square = diff * diff
    folded = square[:, :LANES]
    for j in range(LANES, share, LANES):
        folded = folded + square[:, j : j + LANES]
    err_row = jnp.sum(folded.T, axis=0, keepdims=True)
    parts = pieces(err_row, 3)
    line = lax.broadcasted_iota(jnp.int32, (16, n * count), 0)
    stack = jnp.where(line == 3, 1.0, 0.0)
    for i, part in enumerate(parts):
        stack = jnp.where(line == i, part.astype(F32), stack)
    by_fine = dot(stack.astype(BF), h1r[...])
    err_fine = by_fine[0:1] + by_fine[1:2] + by_fine[2:3]
    for i in range(n):
        err_own[i] = err_fine[:, i * fine_dev : (i + 1) * fine_dev]
        tally[i] = by_fine[3:4, i * fine_dev : (i + 1) * fine_dev]
    err_copies = []
    for k in range(1, n):
        src = err_own.at[lax.rem(me + k, n)]
        err_copies.append(
            remote(src, err_all.at[me], out_send.at[2, k], out_recv.at[2, k], clus_peer(k))
        )
    start(err_copies)
    err_all[me] = err_own[me]
    arrive(err_copies)
    err = err_all[0]
    for i in range(1, n):
        err = err + err_all[i]
    spread_ref[...] = err / (width * (tally[me] + 1.0))
    for copy in local_copies:
        copy.wait()
    arrive(out_copies)
    arrive(fine_copies)
    for copy in started:
        copy.wait_send()


def fused(rows, fine_assign, parent1, parent2, parent3, shrink):
    n = lax.axis_size("clus")
    m = lax.axis_size("dp")
    count, width = rows.shape
    fine_dev = parent1.shape[0]
    middle = parent2.shape[0]
    third = parent3.shape[0]
    share = width // n
    chunks = share // LANES
    pairs = m // 2
    half = LANES // 2
    thin = half // pairs
    fine = n * fine_dev
    total_rows = n * count
    vmem = pl.BlockSpec(memory_space=pltpu.VMEM)
    dma = pltpu.SemaphoreType.DMA
    fine_out, mid_out, coarse_out, spread = pl.pallas_call(
        functools.partial(sweep, n, m),
        out_shape=(
            jax.ShapeDtypeStruct((fine_dev, width), BF),
            jax.ShapeDtypeStruct((middle // n, width), BF),
            jax.ShapeDtypeStruct((third // (n * m), width), BF),
            jax.ShapeDtypeStruct((1, fine_dev), F32),
        ),
        in_specs=[vmem] * 4
        + [pl.BlockSpec(memory_space=pltpu.SMEM), pl.BlockSpec(memory_space=pl.ANY)],
        out_specs=[vmem] * 4,
        scratch_shapes=[
            pltpu.VMEM((n, 1, count), jnp.int32),
            pltpu.VMEM((n, 1, fine_dev), jnp.int32),
            pltpu.VMEM((total_rows, share), BF),
            pltpu.VMEM((fine, total_rows), BF),
            pltpu.VMEM((middle, total_rows), BF),
            pltpu.VMEM((third, total_rows), BF),
            pltpu.VMEM((total_rows, fine), BF),
            pltpu.VMEM((fine, middle), BF),
            pltpu.VMEM((third, middle), BF),
            pltpu.VMEM((fine, share), F32),
            pltpu.VMEM((middle, share), F32),
            pltpu.VMEM((fine, LANES), F32),
            pltpu.VMEM((middle, LANES), F32),
            pltpu.VMEM((chunks, LANES, third), F32),
            pltpu.VMEM((chunks, half, third), F32),
            pltpu.VMEM((chunks, half, third), F32),
            pltpu.VMEM((chunks, pairs, thin, third), F32),
            pltpu.VMEM((1, third), F32),
            pltpu.VMEM((m, 1, third), F32),
            pltpu.VMEM((chunks, LANES, third), BF),
            pltpu.VMEM((fine, share), BF),
            pltpu.VMEM((middle, share), BF),
            pltpu.VMEM((third, share), BF),
            pltpu.VMEM((n, 1, fine_dev), F32),
            pltpu.VMEM((n, 1, fine_dev), F32),
            pltpu.VMEM((n, 1, fine_dev), F32),
            dma((2, n)),
            dma((2, n)),
            dma((chunks, n)),
            dma((chunks, n)),
            dma((chunks,)),
            dma((chunks,)),
            dma((chunks, pairs)),
            dma((chunks, pairs)),
            dma((m,)),
            dma((m,)),
            dma((chunks, pairs)),
            dma((chunks, pairs)),
            dma((chunks,)),
            dma((chunks,)),
            dma((chunks, n)),
            dma((chunks, n)),
            dma((3, n)),
            dma((3, n)),
            dma((3 + chunks,)),
        ],
        compiler_params=pltpu.CompilerParams(
            collective_id=0, has_side_effects=True, vmem_limit_bytes=60 << 20
        ),
        name="sweep",
    )(
        fine_assign.reshape(1, count),
        parent1.reshape(1, fine_dev),
        parent2.reshape(1, middle),
        parent3.reshape(1, third),
        shrink,
        rows,
    )
    return fine_out, mid_out, coarse_out, spread.reshape(fine_dev)


def fits(rows, fine_assign, parent1, parent2, parent3):
    n = lax.axis_size("clus")
    m = lax.axis_size("dp")
    return (
        rows.shape[1] % (n * LANES) == 0
        and m % 2 == 0
        and (LANES // 2) % (m // 2 * 16) == 0
        and rows.shape[0] % LANES == 0
        and parent1.shape[0] % LANES == 0
        and parent2.shape[0] % LANES == 0
        and parent2.shape[0] <= 256
        and parent2.shape[0] % (n * 16) == 0
        and parent3.shape[0] % LANES == 0
        and parent3.shape[0] % (n * m * 16) == 0
    )


def step(rows, fine_assign, parent1, parent2, parent3, shrink):
    form = fused if fits(rows, fine_assign, parent1, parent2, parent3) else local
    return form(rows, fine_assign, parent1, parent2, parent3, shrink)


def solution(mesh):
    placed = (P(("dp", "clus"), None), P(("dp", "clus")), P(("dp", "clus")), P("dp"), P(), P())
    return jax.shard_map(
        step,
        mesh=mesh,
        in_specs=placed,
        out_specs=(
            P(("dp", "clus"), None),
            P(("dp", "clus"), None),
            P(("dp", "clus"), None),
            P(("dp", "clus")),
        ),
        check_vma=False,
    )
```

```python
import functools

import jax
import jax.numpy as jnp
from jax import lax
from jax.experimental import pallas as pl
from jax.experimental.pallas import tpu as pltpu
from jax.sharding import PartitionSpec as P

K4 = 64


HIGH = lax.Precision.HIGHEST


def shrunk(sums, counts, prior, weight):
    return (sums + weight * prior) / (counts + weight)[:, None]


def local(rows, fine_assign, parent1, parent2, parent3, shrink):
    groups = lax.axis_size("clus")
    dp_count = lax.axis_size("dp")
    devices = groups * dp_count
    clus_index = lax.axis_index("clus")
    dp_index = lax.axis_index("dp")
    count = rows.shape[0]
    width = rows.shape[1]
    fine_dev = parent1.shape[0]
    middle_dp = parent2.shape[0]
    third = parent3.shape[0]
    slots = 2 * count // groups
    total = count * devices
    weight_top = shrink[0] * (total / K4)
    weight_third = shrink[1] * (total / third)
    weight_middle = shrink[2] * (total / (middle_dp * dp_count))
    weight_fine = shrink[3] * (total / (fine_dev * devices))
    local_ids = fine_assign - dp_index * groups * fine_dev
    target = local_ids // fine_dev
    within = local_ids - target * fine_dev
    target_hot = (target[:, None] == jnp.arange(groups)[None, :]).astype(jnp.bfloat16)
    earlier = (jnp.arange(count)[:, None] > jnp.arange(count)[None, :]).astype(jnp.bfloat16)
    before = jnp.dot(earlier, target_hot, preferred_element_type=jnp.float32)
    rank = jnp.sum(before * target_hot.astype(jnp.float32), axis=1).astype(jnp.int32)
    slot_of = target * slots + rank
    source = (
        jnp.full((groups * slots,), count, jnp.int32)
        .at[slot_of]
        .set(jnp.arange(count, dtype=jnp.int32))
    )
    padded = jnp.concatenate([rows, jnp.zeros((1, width), jnp.bfloat16)], axis=0)
    send_rows = padded[source].reshape(groups, slots, width)
    send_ids = jnp.concatenate([within, jnp.full((1,), -1, jnp.int32)])[source].reshape(
        groups, slots
    )
    got_rows, got_ids = (
        lax.all_to_all(send_rows, "clus", split_axis=0, concat_axis=0, tiled=True),
        lax.all_to_all(send_ids, "clus", split_axis=0, concat_axis=0, tiled=True),
    )
    got_rows = got_rows.reshape(groups * slots, width)
    got_ids = got_ids.reshape(groups * slots)
    member = (got_ids[:, None] == jnp.arange(fine_dev)[None, :]).astype(jnp.bfloat16)
    contract = (((0,), (0,)), ((), ()))
    fine_sums = lax.dot_general(member, got_rows, contract, preferred_element_type=jnp.float32)
    fine_counts = jnp.sum(member.astype(jnp.float32), axis=0)
    middle_local = parent1 - dp_index * middle_dp
    child_hot = (jnp.arange(middle_dp)[:, None] == middle_local[None, :]).astype(jnp.float32)
    middle_part = jnp.dot(child_hot, fine_sums, precision=HIGH)
    middle_tally = jnp.dot(child_hot, fine_counts, precision=HIGH)
    share = middle_dp // groups
    offset = clus_index * share
    middle_sums, middle_counts = (
        lax.psum_scatter(middle_part, "clus", scatter_dimension=0, tiled=True),
        lax.psum_scatter(middle_tally, "clus", scatter_dimension=0, tiled=True),
    )
    own_parent2 = lax.dynamic_slice_in_dim(parent2, offset, share, 0)
    third_share = third // devices
    third_start = (dp_index * groups + clus_index) * third_share
    third_hot = (jnp.arange(third)[:, None] == own_parent2[None, :]).astype(jnp.float32)
    third_part = jnp.dot(third_hot, middle_sums, precision=HIGH)
    third_tally = jnp.dot(third_hot, middle_counts, precision=HIGH)
    third_sums, third_counts = lax.psum((third_part, third_tally), ("dp", "clus"))
    top_hot = (jnp.arange(K4)[:, None] == parent3[None, :]).astype(jnp.float32)
    top_sums = jnp.dot(top_hot, third_sums, precision=HIGH)
    top_counts = jnp.dot(top_hot, third_counts, precision=HIGH)
    center = jnp.sum(top_sums, axis=0) / total
    top_means = shrunk(top_sums, top_counts, center[None, :], weight_top)
    third_means = shrunk(
        third_sums, third_counts, jnp.dot(top_hot.T, top_means, precision=HIGH), weight_third
    )
    third_out = lax.dynamic_slice_in_dim(third_means, third_start, third_share, 0)
    parent_hot = (own_parent2[:, None] == jnp.arange(third)[None, :]).astype(jnp.float32)
    middle_out = shrunk(
        middle_sums, middle_counts, jnp.dot(parent_hot, third_means, precision=HIGH), weight_middle
    )
    middle_means = lax.all_gather(middle_out, "clus", axis=0, tiled=True)
    fine_means = shrunk(
        fine_sums, fine_counts, jnp.dot(child_hot.T, middle_means, precision=HIGH), weight_fine
    )
    fine_out = fine_means.astype(jnp.bfloat16)
    back = jnp.dot(member, fine_out, preferred_element_type=jnp.float32)
    diff = got_rows.astype(jnp.float32) - back
    row_error = jnp.sum(diff * diff, axis=1)
    spread = jnp.sum(member.astype(jnp.float32) * row_error[:, None], axis=0) / (
        width * (fine_counts + 1.0)
    )
    return (fine_out, middle_out.astype(jnp.bfloat16), third_out.astype(jnp.bfloat16), spread)


LANES = 128
BF = jnp.bfloat16
F32 = jnp.float32
MESH = pl.DeviceIdType.MESH


def rows_hot(size, ids):
    shape = (size, ids.shape[1])
    return jnp.where(lax.broadcasted_iota(jnp.int32, shape, 0) == ids, 1.0, 0.0).astype(BF)


def column_of(ids):
    return jnp.broadcast_to(ids.astype(F32), (LANES, ids.shape[1])).T


def lanes_hot(column, start):
    lane = lax.broadcasted_iota(jnp.int32, column.shape, 1).astype(F32) + float(start)
    return jnp.where(column == lane, 1.0, 0.0).astype(BF)


def dot(a, b):
    return jnp.dot(a, b, preferred_element_type=F32)


def pieces(x, count):
    out = []
    for _ in range(count):
        part = x.astype(BF)
        out.append(part)
        x = x - part.astype(F32)
    return out


def dot_left(x, hot, count=3):
    return sum(dot(part, hot) for part in pieces(x, count))


def sweep(
    n,
    m,
    fa_ref,
    p1_ref,
    p2_ref,
    p3_ref,
    shrink_ref,
    rows_ref,
    fine_ref,
    mid_ref,
    coarse_ref,
    spread_ref,
    fa_all,
    p1_all,
    got,
    h1f,
    h2f,
    h3f,
    h1r,
    h1m,
    h23,
    base1,
    base2,
    pull1,
    pull2,
    part_own,
    pair_got,
    pair_sum,
    part_all,
    cnt_own,
    cnt_all,
    means3,
    fine_own,
    mid_own,
    coarse_own,
    err_own,
    err_all,
    tally,
    id_send,
    id_recv,
    row_send,
    row_recv,
    pair_send,
    pair_recv,
    part_send,
    part_recv,
    cnt_send,
    cnt_recv,
    back_send,
    back_recv,
    relay_send,
    relay_recv,
    fine_send,
    fine_recv,
    out_send,
    out_recv,
    local_sem,
):
    me = lax.axis_index("clus")
    dp = lax.axis_index("dp")
    count, width = rows_ref.shape
    share = width // n
    chunks = share // LANES
    fine_dev = p1_ref.shape[1]
    middle = p2_ref.shape[1]
    third = p3_ref.shape[1]
    devices = n * m
    total = count * devices
    fine = n * fine_dev
    pairs = m // 2
    half = LANES // 2
    thin = half // pairs
    pair = dp // 2
    side = lax.rem(dp, 2)
    mid_share = middle // n
    third_share = third // devices
    w4 = shrink_ref[0] * (total / K4)
    w3 = shrink_ref[1] * (total / third)
    w2 = shrink_ref[2] * (total / (middle * m))
    w1 = shrink_ref[3] * (total / (fine_dev * devices))

    def span(index, size):
        return pl.ds(pl.multiple_of(index * size, size), size)

    def chunk_of(h):
        return slice(h * LANES, (h + 1) * LANES)

    def remote(src, dst, send, recv, device):
        return pltpu.make_async_remote_copy(
            src_ref=src,
            dst_ref=dst,
            send_sem=send,
            recv_sem=recv,
            device_id=device,
            device_id_type=MESH,
        )

    def clus_peer(k):
        return {"clus": lax.rem(me + k, n)}

    def dp_peer(k):
        return {"dp": lax.rem(dp + k, m)}

    def pair_peer(k):
        return {"dp": lax.rem(pair + k, pairs) * 2 + side}

    other = {"dp": pair * 2 + 1 - side}

    started = []

    def start(copies):
        for copy in copies:
            copy.start()
        started.extend(copies)
        return copies

    def arrive(copies):
        for copy in copies:
            copy.wait_recv()

    barrier = pltpu.get_barrier_semaphore()
    for k in range(1, n):
        pl.semaphore_signal(barrier, inc=1, device_id=clus_peer(k), device_id_type=MESH)
    for k in range(1, m):
        pl.semaphore_signal(barrier, inc=1, device_id=dp_peer(k), device_id_type=MESH)
    own_rows = pltpu.make_async_copy(
        rows_ref.at[:, span(me, share)], got.at[span(me, count), :], local_sem.at[0]
    )
    own_rows.start()
    fa_all[me] = fa_ref[...]
    p1_all[me] = p1_ref[...]
    p2_row = p2_ref[...]
    p3_row = p3_ref[...]
    pl.semaphore_wait(barrier, n - 1 + m - 1)

    id_copies = []
    for k in range(1, n):
        for which, (src, dst) in enumerate(((fa_ref, fa_all), (p1_ref, p1_all))):
            id_copies.append(
                remote(src, dst.at[me], id_send.at[which, k], id_recv.at[which, k], clus_peer(k))
            )
    start(id_copies)
    row_copies = []
    for h in range(chunks):
        copies = []
        for k in range(1, n):
            column = lax.rem(me + k, n) * share + h * LANES
            copies.append(
                remote(
                    rows_ref.at[:, pl.ds(pl.multiple_of(column, LANES), LANES)],
                    got.at[span(me, count), chunk_of(h)],
                    row_send.at[h, k],
                    row_recv.at[h, k],
                    clus_peer(k),
                )
            )
        row_copies.append(start(copies))

    h23[...] = rows_hot(third, p2_row)
    h4 = lanes_hot(column_of(p3_row), 0)
    h4f = rows_hot(LANES, p3_row)
    high = p2_row // 256
    top_line = lax.broadcasted_iota(jnp.int32, (16, middle), 0) == 0
    p2_split = jnp.where(top_line, high, p2_row - high * 256).astype(F32).astype(BF)

    arrive(id_copies)
    fa_row = jnp.concatenate([fa_all[i] for i in range(n)], axis=1) - dp * fine
    p1_row = jnp.concatenate([p1_all[i] for i in range(n)], axis=1) - dp * middle
    h1f[...] = rows_hot(fine, fa_row)
    p1_lines = jnp.broadcast_to(p1_row, (16, fine)).astype(F32).astype(BF)
    mid_row = dot(p1_lines, h1f[...])[0:1].astype(jnp.int32)
    h2f[...] = rows_hot(middle, mid_row)
    halves = dot(p2_split, h2f[...])
    third_row = (halves[0:1] * 256.0 + halves[1:2]).astype(jnp.int32)
    h3f[...] = rows_hot(third, third_row)
    ones = jnp.ones((n * count, LANES), BF)
    own_rows.wait()

    pair_copies = []
    part_copies = []
    back_copies = []
    relay_copies = []
    cnt_copies = []

    def sum_part(h):
        arrive(row_copies[h])
        part_own[h] = dot(h3f[...], got[:, chunk_of(h)]).T
        away = part_own.at[h, span(1 - side, half), :]
        copy = remote(away, pair_got.at[h], pair_send.at[h], pair_recv.at[h], other)
        pair_copies.append(start([copy]))

    def sum_pair(h):
        arrive(pair_copies[h])
        pair_sum[h] = part_own[h, span(side, half), :] + pair_got[h]
        copies = []
        for k in range(1, pairs):
            copies.append(
                remote(
                    pair_sum.at[h, span(lax.rem(pair + k, pairs), thin), :],
                    part_all.at[h, pair],
                    part_send.at[h, k],
                    part_recv.at[h, k],
                    pair_peer(k),
                )
            )
        part_copies.append(start(copies))
        part_all[h, pair] = pair_sum[h, span(pair, thin), :]

    def third_level(h, cnt3, cnt4):
        arrive(part_copies[h])
        sums3 = part_all[h, 0]
        for i in range(1, pairs):
            sums3 = sums3 + part_all[h, i]
        sums4 = dot_left(sums3, h4)
        center = jnp.sum(sums4, axis=1, keepdims=True) / total
        means4 = (sums4 + w4 * center) / (cnt4 + w4)
        place = span(side * pairs + pair, thin)
        means3[h, place, :] = ((sums3 + w3 * dot_left(means4, h4f)) / (cnt3 + w3)).astype(BF)
        copies = []
        for k in range(1, pairs):
            block = means3.at[h, place, :]
            copies.append(remote(block, block, back_send.at[h, k], back_recv.at[h, k], pair_peer(k)))
        back_copies.append(start(copies))

    def relay(h):
        arrive(back_copies[h])
        block = means3.at[h, span(side, half), :]
        copy = remote(block, block, relay_send.at[h], relay_recv.at[h], other)
        relay_copies.append(start([copy]))

    sum_part(0)
    cnt_part = dot(h3f[...], ones).T[0:1]
    cnt_own[...] = cnt_part
    cnt_all[dp] = cnt_part
    for k in range(1, m):
        cnt_copies.append(
            remote(cnt_own, cnt_all.at[dp], cnt_send.at[k], cnt_recv.at[k], dp_peer(k))
        )
    start(cnt_copies)
    p1_column = column_of(p1_row)
    for j in range(0, middle, LANES):
        h1m[:, j : j + LANES] = lanes_hot(p1_column, j)
    for h in range(1, chunks):
        sum_pair(h - 1)
        sum_part(h)
    scale1 = 1.0 / (dot(h1f[...], ones) + w1)
    scale2 = 1.0 / (dot(h2f[...], ones) + w2)
    pull1[...] = w1 * scale1
    pull2[...] = w2 * scale2
    sum_pair(chunks - 1)
    for h in range(chunks):
        base1[:, chunk_of(h)] = dot(h1f[...], got[:, chunk_of(h)]) * scale1
        base2[:, chunk_of(h)] = dot(h2f[...], got[:, chunk_of(h)]) * scale2
    arrive(cnt_copies)
    cnt3 = cnt_all[0]
    for i in range(1, m):
        cnt3 = cnt3 + cnt_all[i]
    cnt4 = dot_left(jnp.broadcast_to(cnt3, (16, third)), h4)[0:1]
    for h in range(chunks):
        third_level(h, cnt3, cnt4)
    fa_column = column_of(fa_row)
    for j in range(0, fine, LANES):
        h1r[:, j : j + LANES] = lanes_hot(fa_column, j)
    fine_copies = []
    local_copies = []
    for h in range(chunks):
        relay(h)
        arrive(relay_copies[h])
        columns = pl.ds(pl.multiple_of(me * share + h * LANES, LANES), LANES)
        means2 = base2[:, chunk_of(h)] + pull2[...] * dot(means3[h], h23[...]).T
        mid_own[:, chunk_of(h)] = means2.astype(BF)
        parts = pieces(means2, 2)
        for k in (*range(1, n), 0):
            block = span(lax.rem(me + k, n), fine_dev)
            prior = sum(dot(h1m[block, :], part) for part in parts)
            means1 = base1[block, chunk_of(h)] + pull1[block, :] * prior
            fine_own[block, chunk_of(h)] = means1.astype(BF)
            src = fine_own.at[block, chunk_of(h)]
            dst = fine_ref.at[:, columns]
            if k:
                copy = remote(src, dst, fine_send.at[h, k], fine_recv.at[h, k], clus_peer(k))
                fine_copies.extend(start([copy]))
            else:
                copy = pltpu.make_async_copy(src, dst, local_sem.at[3 + h])
                copy.start()
                local_copies.append(copy)
    for h in range(chunks):
        coarse_own[:, chunk_of(h)] = means3[h].astype(F32).T.astype(BF)
    columns = span(me, share)
    out_copies = []
    plan = (
        (mid_own, mid_ref, lambda peer: span(peer, mid_share)),
        (coarse_own, coarse_ref, lambda peer: span(dp * n + peer, third_share)),
    )
    for which, (src, dst, place) in enumerate(plan):
        for k in range(1, n):
            out_copies.append(
                remote(
                    src.at[place(lax.rem(me + k, n)), :],
                    dst.at[:, columns],
                    out_send.at[which, k],
                    out_recv.at[which, k],
                    clus_peer(k),
                )
            )
        copy = pltpu.make_async_copy(
            src.at[place(me), :], dst.at[:, columns], local_sem.at[1 + which]
        )
        copy.start()
        local_copies.append(copy)
    start(out_copies)

    diff = got[...].astype(F32) - dot(h1r[...], fine_own[...])
    square = diff * diff
    folded = square[:, :LANES]
    for j in range(LANES, share, LANES):
        folded = folded + square[:, j : j + LANES]
    err_row = jnp.sum(folded.T, axis=0, keepdims=True)
    parts = pieces(err_row, 3)
    line = lax.broadcasted_iota(jnp.int32, (16, n * count), 0)
    stack = jnp.where(line == 3, 1.0, 0.0)
    for i, part in enumerate(parts):
        stack = jnp.where(line == i, part.astype(F32), stack)
    by_fine = dot(stack.astype(BF), h1r[...])
    err_fine = by_fine[0:1] + by_fine[1:2] + by_fine[2:3]
    for i in range(n):
        err_own[i] = err_fine[:, i * fine_dev : (i + 1) * fine_dev]
        tally[i] = by_fine[3:4, i * fine_dev : (i + 1) * fine_dev]
    err_copies = []
    for k in range(1, n):
        src = err_own.at[lax.rem(me + k, n)]
        err_copies.append(
            remote(src, err_all.at[me], out_send.at[2, k], out_recv.at[2, k], clus_peer(k))
        )
    start(err_copies)
    err_all[me] = err_own[me]
    arrive(err_copies)
    err = err_all[0]
    for i in range(1, n):
        err = err + err_all[i]
    spread_ref[...] = err / (width * (tally[me] + 1.0))
    for copy in local_copies:
        copy.wait()
    arrive(out_copies)
    arrive(fine_copies)
    for copy in started:
        copy.wait_send()


def land(count, *refs):
    sem = refs[-1]
    pairs = zip(refs[:count], refs[count : 2 * count])
    copies = [pltpu.make_async_copy(a, b, sem.at[i]) for i, (a, b) in enumerate(pairs)]
    for copy in copies:
        copy.start()
    for copy in copies:
        copy.wait()


def settle(*arrays):
    count = len(arrays)
    return pl.pallas_call(
        functools.partial(land, count),
        out_shape=tuple(jax.ShapeDtypeStruct(a.shape, a.dtype) for a in arrays),
        in_specs=[pl.BlockSpec(memory_space=pltpu.VMEM)] * count,
        out_specs=tuple([pl.BlockSpec(memory_space=pl.ANY)] * count),
        scratch_shapes=[pltpu.SemaphoreType.DMA((count,))],
        compiler_params=pltpu.CompilerParams(vmem_limit_bytes=4 << 20),
        name="settle",
    )(*arrays)


def fused(rows, fine_assign, parent1, parent2, parent3, shrink):
    n = lax.axis_size("clus")
    m = lax.axis_size("dp")
    count, width = rows.shape
    fine_dev = parent1.shape[0]
    middle = parent2.shape[0]
    third = parent3.shape[0]
    share = width // n
    chunks = share // LANES
    pairs = m // 2
    half = LANES // 2
    thin = half // pairs
    fine = n * fine_dev
    total_rows = n * count
    vmem = pl.BlockSpec(memory_space=pltpu.VMEM)
    dma = pltpu.SemaphoreType.DMA
    fine_out, mid_out, coarse_out, spread = pl.pallas_call(
        functools.partial(sweep, n, m),
        out_shape=(
            jax.ShapeDtypeStruct((fine_dev, width), BF),
            jax.ShapeDtypeStruct((middle // n, width), BF),
            jax.ShapeDtypeStruct((third // (n * m), width), BF),
            jax.ShapeDtypeStruct((1, fine_dev), F32),
        ),
        in_specs=[vmem] * 4
        + [pl.BlockSpec(memory_space=pltpu.SMEM), pl.BlockSpec(memory_space=pltpu.HBM)],
        out_specs=[vmem] * 4,
        scratch_shapes=[
            pltpu.VMEM((n, 1, count), jnp.int32),
            pltpu.VMEM((n, 1, fine_dev), jnp.int32),
            pltpu.VMEM((total_rows, share), BF),
            pltpu.VMEM((fine, total_rows), BF),
            pltpu.VMEM((middle, total_rows), BF),
            pltpu.VMEM((third, total_rows), BF),
            pltpu.VMEM((total_rows, fine), BF),
            pltpu.VMEM((fine, middle), BF),
            pltpu.VMEM((third, middle), BF),
            pltpu.VMEM((fine, share), F32),
            pltpu.VMEM((middle, share), F32),
            pltpu.VMEM((fine, LANES), F32),
            pltpu.VMEM((middle, LANES), F32),
            pltpu.VMEM((chunks, LANES, third), F32),
            pltpu.VMEM((chunks, half, third), F32),
            pltpu.VMEM((chunks, half, third), F32),
            pltpu.VMEM((chunks, pairs, thin, third), F32),
            pltpu.VMEM((1, third), F32),
            pltpu.VMEM((m, 1, third), F32),
            pltpu.VMEM((chunks, LANES, third), BF),
            pltpu.VMEM((fine, share), BF),
            pltpu.VMEM((middle, share), BF),
            pltpu.VMEM((third, share), BF),
            pltpu.VMEM((n, 1, fine_dev), F32),
            pltpu.VMEM((n, 1, fine_dev), F32),
            pltpu.VMEM((n, 1, fine_dev), F32),
            dma((2, n)),
            dma((2, n)),
            dma((chunks, n)),
            dma((chunks, n)),
            dma((chunks,)),
            dma((chunks,)),
            dma((chunks, pairs)),
            dma((chunks, pairs)),
            dma((m,)),
            dma((m,)),
            dma((chunks, pairs)),
            dma((chunks, pairs)),
            dma((chunks,)),
            dma((chunks,)),
            dma((chunks, n)),
            dma((chunks, n)),
            dma((3, n)),
            dma((3, n)),
            dma((3 + chunks,)),
        ],
        compiler_params=pltpu.CompilerParams(
            collective_id=0, has_side_effects=True, vmem_limit_bytes=32 << 20
        ),
        name="sweep",
    )(
        fine_assign.reshape(1, count),
        parent1.reshape(1, fine_dev),
        parent2.reshape(1, middle),
        parent3.reshape(1, third),
        shrink,
        rows,
    )
    fine_out, mid_out, coarse_out, spread = settle(fine_out, mid_out, coarse_out, spread)
    return fine_out, mid_out, coarse_out, spread.reshape(fine_dev)


def fits(rows, fine_assign, parent1, parent2, parent3):
    n = lax.axis_size("clus")
    m = lax.axis_size("dp")
    return (
        rows.shape[1] % (n * LANES) == 0
        and m % 2 == 0
        and (LANES // 2) % (m // 2 * 16) == 0
        and rows.shape[0] % LANES == 0
        and parent1.shape[0] % LANES == 0
        and parent2.shape[0] % LANES == 0
        and parent2.shape[0] <= 256
        and parent2.shape[0] % (n * 16) == 0
        and parent3.shape[0] % LANES == 0
        and parent3.shape[0] % (n * m * 16) == 0
    )


def step(rows, fine_assign, parent1, parent2, parent3, shrink):
    form = fused if fits(rows, fine_assign, parent1, parent2, parent3) else local
    return form(rows, fine_assign, parent1, parent2, parent3, shrink)


def solution(mesh):
    placed = (P(("dp", "clus"), None), P(("dp", "clus")), P(("dp", "clus")), P("dp"), P(), P())
    return jax.shard_map(
        step,
        mesh=mesh,
        in_specs=placed,
        out_specs=(
            P(("dp", "clus"), None),
            P(("dp", "clus"), None),
            P(("dp", "clus"), None),
            P(("dp", "clus")),
        ),
        check_vma=False,
    )
```

```python
import functools

import jax
import jax.numpy as jnp
from jax import lax
from jax.experimental import pallas as pl
from jax.experimental.pallas import tpu as pltpu
from jax.sharding import PartitionSpec as P

K4 = 64


HIGH = lax.Precision.HIGHEST


def shrunk(sums, counts, prior, weight):
    return (sums + weight * prior) / (counts + weight)[:, None]


def local(rows, fine_assign, parent1, parent2, parent3, shrink):
    groups = lax.axis_size("clus")
    dp_count = lax.axis_size("dp")
    devices = groups * dp_count
    clus_index = lax.axis_index("clus")
    dp_index = lax.axis_index("dp")
    count = rows.shape[0]
    width = rows.shape[1]
    fine_dev = parent1.shape[0]
    middle_dp = parent2.shape[0]
    third = parent3.shape[0]
    slots = 2 * count // groups
    total = count * devices
    weight_top = shrink[0] * (total / K4)
    weight_third = shrink[1] * (total / third)
    weight_middle = shrink[2] * (total / (middle_dp * dp_count))
    weight_fine = shrink[3] * (total / (fine_dev * devices))
    local_ids = fine_assign - dp_index * groups * fine_dev
    target = local_ids // fine_dev
    within = local_ids - target * fine_dev
    target_hot = (target[:, None] == jnp.arange(groups)[None, :]).astype(jnp.bfloat16)
    earlier = (jnp.arange(count)[:, None] > jnp.arange(count)[None, :]).astype(jnp.bfloat16)
    before = jnp.dot(earlier, target_hot, preferred_element_type=jnp.float32)
    rank = jnp.sum(before * target_hot.astype(jnp.float32), axis=1).astype(jnp.int32)
    slot_of = target * slots + rank
    source = (
        jnp.full((groups * slots,), count, jnp.int32)
        .at[slot_of]
        .set(jnp.arange(count, dtype=jnp.int32))
    )
    padded = jnp.concatenate([rows, jnp.zeros((1, width), jnp.bfloat16)], axis=0)
    send_rows = padded[source].reshape(groups, slots, width)
    send_ids = jnp.concatenate([within, jnp.full((1,), -1, jnp.int32)])[source].reshape(
        groups, slots
    )
    got_rows, got_ids = (
        lax.all_to_all(send_rows, "clus", split_axis=0, concat_axis=0, tiled=True),
        lax.all_to_all(send_ids, "clus", split_axis=0, concat_axis=0, tiled=True),
    )
    got_rows = got_rows.reshape(groups * slots, width)
    got_ids = got_ids.reshape(groups * slots)
    member = (got_ids[:, None] == jnp.arange(fine_dev)[None, :]).astype(jnp.bfloat16)
    contract = (((0,), (0,)), ((), ()))
    fine_sums = lax.dot_general(member, got_rows, contract, preferred_element_type=jnp.float32)
    fine_counts = jnp.sum(member.astype(jnp.float32), axis=0)
    middle_local = parent1 - dp_index * middle_dp
    child_hot = (jnp.arange(middle_dp)[:, None] == middle_local[None, :]).astype(jnp.float32)
    middle_part = jnp.dot(child_hot, fine_sums, precision=HIGH)
    middle_tally = jnp.dot(child_hot, fine_counts, precision=HIGH)
    share = middle_dp // groups
    offset = clus_index * share
    middle_sums, middle_counts = (
        lax.psum_scatter(middle_part, "clus", scatter_dimension=0, tiled=True),
        lax.psum_scatter(middle_tally, "clus", scatter_dimension=0, tiled=True),
    )
    own_parent2 = lax.dynamic_slice_in_dim(parent2, offset, share, 0)
    third_share = third // devices
    third_start = (dp_index * groups + clus_index) * third_share
    third_hot = (jnp.arange(third)[:, None] == own_parent2[None, :]).astype(jnp.float32)
    third_part = jnp.dot(third_hot, middle_sums, precision=HIGH)
    third_tally = jnp.dot(third_hot, middle_counts, precision=HIGH)
    third_sums, third_counts = lax.psum((third_part, third_tally), ("dp", "clus"))
    top_hot = (jnp.arange(K4)[:, None] == parent3[None, :]).astype(jnp.float32)
    top_sums = jnp.dot(top_hot, third_sums, precision=HIGH)
    top_counts = jnp.dot(top_hot, third_counts, precision=HIGH)
    center = jnp.sum(top_sums, axis=0) / total
    top_means = shrunk(top_sums, top_counts, center[None, :], weight_top)
    third_means = shrunk(
        third_sums, third_counts, jnp.dot(top_hot.T, top_means, precision=HIGH), weight_third
    )
    third_out = lax.dynamic_slice_in_dim(third_means, third_start, third_share, 0)
    parent_hot = (own_parent2[:, None] == jnp.arange(third)[None, :]).astype(jnp.float32)
    middle_out = shrunk(
        middle_sums, middle_counts, jnp.dot(parent_hot, third_means, precision=HIGH), weight_middle
    )
    middle_means = lax.all_gather(middle_out, "clus", axis=0, tiled=True)
    fine_means = shrunk(
        fine_sums, fine_counts, jnp.dot(child_hot.T, middle_means, precision=HIGH), weight_fine
    )
    fine_out = fine_means.astype(jnp.bfloat16)
    back = jnp.dot(member, fine_out, preferred_element_type=jnp.float32)
    diff = got_rows.astype(jnp.float32) - back
    row_error = jnp.sum(diff * diff, axis=1)
    spread = jnp.sum(member.astype(jnp.float32) * row_error[:, None], axis=0) / (
        width * (fine_counts + 1.0)
    )
    return (fine_out, middle_out.astype(jnp.bfloat16), third_out.astype(jnp.bfloat16), spread)


LANES = 128
BF = jnp.bfloat16
F32 = jnp.float32
MESH = pl.DeviceIdType.MESH


def rows_hot(size, ids):
    shape = (size, ids.shape[1])
    return jnp.where(lax.broadcasted_iota(jnp.int32, shape, 0) == ids, 1.0, 0.0).astype(BF)


def column_of(ids):
    return jnp.broadcast_to(ids.astype(F32), (LANES, ids.shape[1])).T


def lanes_hot(column, start):
    lane = lax.broadcasted_iota(jnp.int32, column.shape, 1).astype(F32) + float(start)
    return jnp.where(column == lane, 1.0, 0.0).astype(BF)


def dot(a, b):
    return jnp.dot(a, b, preferred_element_type=F32)


def pieces(x, count):
    out = []
    for _ in range(count):
        part = x.astype(BF)
        out.append(part)
        x = x - part.astype(F32)
    return out


def dot_left(x, hot, count=3):
    return sum(dot(part, hot) for part in pieces(x, count))


def sweep(
    n,
    m,
    fa_ref,
    p1_ref,
    p2_ref,
    p3_ref,
    shrink_ref,
    rows_ref,
    fine_ref,
    mid_ref,
    coarse_ref,
    spread_ref,
    fa_all,
    p1_all,
    got,
    h1f,
    h2f,
    h3f,
    h1r,
    h1m,
    h23,
    base1,
    base2,
    pull1,
    pull2,
    part_own,
    pair_got,
    pair_sum,
    part_all,
    cnt_own,
    cnt_all,
    means3,
    fine_own,
    mid_own,
    coarse_own,
    err_own,
    err_all,
    tally,
    id_send,
    id_recv,
    row_send,
    row_recv,
    pair_send,
    pair_recv,
    part_send,
    part_recv,
    cnt_send,
    cnt_recv,
    back_send,
    back_recv,
    relay_send,
    relay_recv,
    fine_send,
    fine_recv,
    out_send,
    out_recv,
    local_sem,
):
    me = lax.axis_index("clus")
    dp = lax.axis_index("dp")
    count, width = rows_ref.shape
    share = width // n
    chunks = share // LANES
    fine_dev = p1_ref.shape[1]
    middle = p2_ref.shape[1]
    third = p3_ref.shape[1]
    devices = n * m
    total = count * devices
    fine = n * fine_dev
    pairs = m // 2
    half = LANES // 2
    thin = half // pairs
    pair = dp // 2
    side = lax.rem(dp, 2)
    mid_share = middle // n
    third_share = third // devices
    w4 = shrink_ref[0] * (total / K4)
    w3 = shrink_ref[1] * (total / third)
    w2 = shrink_ref[2] * (total / (middle * m))
    w1 = shrink_ref[3] * (total / (fine_dev * devices))

    def span(index, size):
        return pl.ds(pl.multiple_of(index * size, size), size)

    def chunk_of(h):
        return slice(h * LANES, (h + 1) * LANES)

    def remote(src, dst, send, recv, device):
        return pltpu.make_async_remote_copy(
            src_ref=src,
            dst_ref=dst,
            send_sem=send,
            recv_sem=recv,
            device_id=device,
            device_id_type=MESH,
        )

    def clus_peer(k):
        return {"clus": lax.rem(me + k, n)}

    def dp_peer(k):
        return {"dp": lax.rem(dp + k, m)}

    def pair_peer(k):
        return {"dp": lax.rem(pair + k, pairs) * 2 + side}

    other = {"dp": pair * 2 + 1 - side}

    started = []

    def start(copies):
        for copy in copies:
            copy.start()
        started.extend(copies)
        return copies

    def arrive(copies):
        for copy in copies:
            copy.wait_recv()

    barrier = pltpu.get_barrier_semaphore()
    for k in range(1, n):
        pl.semaphore_signal(barrier, inc=1, device_id=clus_peer(k), device_id_type=MESH)
    for k in range(1, m):
        pl.semaphore_signal(barrier, inc=1, device_id=dp_peer(k), device_id_type=MESH)
    own_rows = pltpu.make_async_copy(
        rows_ref.at[:, span(me, share)], got.at[span(me, count), :], local_sem.at[0]
    )
    own_rows.start()
    fa_all[me] = fa_ref[...]
    p1_all[me] = p1_ref[...]
    p2_row = p2_ref[...]
    p3_row = p3_ref[...]
    pl.semaphore_wait(barrier, n - 1 + m - 1)

    id_copies = []
    for k in range(1, n):
        for which, (src, dst) in enumerate(((fa_ref, fa_all), (p1_ref, p1_all))):
            id_copies.append(
                remote(src, dst.at[me], id_send.at[which, k], id_recv.at[which, k], clus_peer(k))
            )
    start(id_copies)
    row_copies = []
    for h in range(chunks):
        copies = []
        for k in range(1, n):
            column = lax.rem(me + k, n) * share + h * LANES
            copies.append(
                remote(
                    rows_ref.at[:, pl.ds(pl.multiple_of(column, LANES), LANES)],
                    got.at[span(me, count), chunk_of(h)],
                    row_send.at[h, k],
                    row_recv.at[h, k],
                    clus_peer(k),
                )
            )
        row_copies.append(start(copies))

    h23[...] = rows_hot(third, p2_row)
    h4 = lanes_hot(column_of(p3_row), 0)
    h4f = rows_hot(LANES, p3_row)
    high = p2_row // 256
    top_line = lax.broadcasted_iota(jnp.int32, (16, middle), 0) == 0
    p2_split = jnp.where(top_line, high, p2_row - high * 256).astype(F32).astype(BF)

    arrive(id_copies)
    fa_row = jnp.concatenate([fa_all[i] for i in range(n)], axis=1) - dp * fine
    p1_row = jnp.concatenate([p1_all[i] for i in range(n)], axis=1) - dp * middle
    h1f[...] = rows_hot(fine, fa_row)
    p1_lines = jnp.broadcast_to(p1_row, (16, fine)).astype(F32).astype(BF)
    mid_row = dot(p1_lines, h1f[...])[0:1].astype(jnp.int32)
    h2f[...] = rows_hot(middle, mid_row)
    halves = dot(p2_split, h2f[...])
    third_row = (halves[0:1] * 256.0 + halves[1:2]).astype(jnp.int32)
    h3f[...] = rows_hot(third, third_row)
    ones = jnp.ones((n * count, LANES), BF)
    own_rows.wait()

    pair_copies = []
    part_copies = []
    back_copies = []
    relay_copies = []
    cnt_copies = []

    def sum_part(h):
        arrive(row_copies[h])
        part_own[h] = dot(h3f[...], got[:, chunk_of(h)]).T
        away = part_own.at[h, span(1 - side, half), :]
        copy = remote(away, pair_got.at[h], pair_send.at[h], pair_recv.at[h], other)
        pair_copies.append(start([copy]))

    def sum_pair(h):
        arrive(pair_copies[h])
        pair_sum[h] = part_own[h, span(side, half), :] + pair_got[h]
        copies = []
        for k in range(1, pairs):
            copies.append(
                remote(
                    pair_sum.at[h, span(lax.rem(pair + k, pairs), thin), :],
                    part_all.at[h, pair],
                    part_send.at[h, k],
                    part_recv.at[h, k],
                    pair_peer(k),
                )
            )
        part_copies.append(start(copies))
        part_all[h, pair] = pair_sum[h, span(pair, thin), :]

    def third_level(h, cnt3, cnt4):
        arrive(part_copies[h])
        sums3 = part_all[h, 0]
        for i in range(1, pairs):
            sums3 = sums3 + part_all[h, i]
        sums4 = dot_left(sums3, h4)
        center = jnp.sum(sums4, axis=1, keepdims=True) / total
        means4 = (sums4 + w4 * center) / (cnt4 + w4)
        place = span(side * pairs + pair, thin)
        means3[h, place, :] = ((sums3 + w3 * dot_left(means4, h4f)) / (cnt3 + w3)).astype(BF)
        copies = []
        for k in range(1, pairs):
            block = means3.at[h, place, :]
            copies.append(remote(block, block, back_send.at[h, k], back_recv.at[h, k], pair_peer(k)))
        back_copies.append(start(copies))

    def relay(h):
        arrive(back_copies[h])
        block = means3.at[h, span(side, half), :]
        copy = remote(block, block, relay_send.at[h], relay_recv.at[h], other)
        relay_copies.append(start([copy]))

    sum_part(0)
    cnt_part = dot(h3f[...], ones).T[0:1]
    cnt_own[...] = cnt_part
    cnt_all[dp] = cnt_part
    for k in range(1, m):
        cnt_copies.append(
            remote(cnt_own, cnt_all.at[dp], cnt_send.at[k], cnt_recv.at[k], dp_peer(k))
        )
    start(cnt_copies)
    p1_column = column_of(p1_row)
    for j in range(0, middle, LANES):
        h1m[:, j : j + LANES] = lanes_hot(p1_column, j)
    for h in range(1, chunks):
        sum_pair(h - 1)
        sum_part(h)
    scale1 = 1.0 / (dot(h1f[...], ones) + w1)
    scale2 = 1.0 / (dot(h2f[...], ones) + w2)
    pull1[...] = w1 * scale1
    pull2[...] = w2 * scale2
    sum_pair(chunks - 1)
    for h in range(chunks):
        base1[:, chunk_of(h)] = dot(h1f[...], got[:, chunk_of(h)]) * scale1
        base2[:, chunk_of(h)] = dot(h2f[...], got[:, chunk_of(h)]) * scale2
    arrive(cnt_copies)
    cnt3 = cnt_all[0]
    for i in range(1, m):
        cnt3 = cnt3 + cnt_all[i]
    cnt4 = dot_left(jnp.broadcast_to(cnt3, (16, third)), h4)[0:1]
    for h in range(chunks):
        third_level(h, cnt3, cnt4)
    fa_column = column_of(fa_row)
    for j in range(0, fine, LANES):
        h1r[:, j : j + LANES] = lanes_hot(fa_column, j)
    fine_copies = []
    local_copies = []
    for h in range(chunks):
        relay(h)
        arrive(relay_copies[h])
        columns = pl.ds(pl.multiple_of(me * share + h * LANES, LANES), LANES)
        means2 = base2[:, chunk_of(h)] + pull2[...] * dot(means3[h], h23[...]).T
        mid_own[:, chunk_of(h)] = means2.astype(BF)
        parts = pieces(means2, 2)
        for k in (*range(1, n), 0):
            block = span(lax.rem(me + k, n), fine_dev)
            prior = sum(dot(h1m[block, :], part) for part in parts)
            means1 = base1[block, chunk_of(h)] + pull1[block, :] * prior
            fine_own[block, chunk_of(h)] = means1.astype(BF)
            src = fine_own.at[block, chunk_of(h)]
            dst = fine_ref.at[:, columns]
            if k:
                copy = remote(src, dst, fine_send.at[h, k], fine_recv.at[h, k], clus_peer(k))
                fine_copies.extend(start([copy]))
            else:
                copy = pltpu.make_async_copy(src, dst, local_sem.at[3 + h])
                copy.start()
                local_copies.append(copy)
    for h in range(chunks):
        coarse_own[:, chunk_of(h)] = means3[h].astype(F32).T.astype(BF)
    columns = span(me, share)
    out_copies = []
    plan = (
        (mid_own, mid_ref, lambda peer: span(peer, mid_share)),
        (coarse_own, coarse_ref, lambda peer: span(dp * n + peer, third_share)),
    )
    for which, (src, dst, place) in enumerate(plan):
        for k in range(1, n):
            out_copies.append(
                remote(
                    src.at[place(lax.rem(me + k, n)), :],
                    dst.at[:, columns],
                    out_send.at[which, k],
                    out_recv.at[which, k],
                    clus_peer(k),
                )
            )
        copy = pltpu.make_async_copy(
            src.at[place(me), :], dst.at[:, columns], local_sem.at[1 + which]
        )
        copy.start()
        local_copies.append(copy)
    start(out_copies)

    diff = got[...].astype(F32) - dot(h1r[...], fine_own[...])
    square = diff * diff
    folded = square[:, :LANES]
    for j in range(LANES, share, LANES):
        folded = folded + square[:, j : j + LANES]
    err_row = jnp.sum(folded.T, axis=0, keepdims=True)
    parts = pieces(err_row, 3)
    line = lax.broadcasted_iota(jnp.int32, (16, n * count), 0)
    stack = jnp.where(line == 3, 1.0, 0.0)
    for i, part in enumerate(parts):
        stack = jnp.where(line == i, part.astype(F32), stack)
    by_fine = dot(stack.astype(BF), h1r[...])
    err_fine = by_fine[0:1] + by_fine[1:2] + by_fine[2:3]
    for i in range(n):
        err_own[i] = err_fine[:, i * fine_dev : (i + 1) * fine_dev]
        tally[i] = by_fine[3:4, i * fine_dev : (i + 1) * fine_dev]
    err_copies = []
    for k in range(1, n):
        src = err_own.at[lax.rem(me + k, n)]
        err_copies.append(
            remote(src, err_all.at[me], out_send.at[2, k], out_recv.at[2, k], clus_peer(k))
        )
    start(err_copies)
    err_all[me] = err_own[me]
    arrive(err_copies)
    err = err_all[0]
    for i in range(1, n):
        err = err + err_all[i]
    spread_ref[...] = err / (width * (tally[me] + 1.0))
    for copy in local_copies:
        copy.wait()
    arrive(out_copies)
    arrive(fine_copies)
    for copy in started:
        copy.wait_send()


def land(count, *refs):
    sem = refs[-1]
    pairs = zip(refs[:count], refs[count : 2 * count])
    copies = [pltpu.make_async_copy(a, b, sem.at[i]) for i, (a, b) in enumerate(pairs)]
    for copy in copies:
        copy.start()
    for copy in copies:
        copy.wait()


def settle(*arrays):
    count = len(arrays)
    return pl.pallas_call(
        functools.partial(land, count),
        out_shape=tuple(jax.ShapeDtypeStruct(a.shape, a.dtype) for a in arrays),
        in_specs=[pl.BlockSpec(memory_space=pltpu.VMEM)] * count,
        out_specs=tuple([pl.BlockSpec(memory_space=pl.ANY)] * count),
        scratch_shapes=[pltpu.SemaphoreType.DMA((count,))],
        compiler_params=pltpu.CompilerParams(vmem_limit_bytes=4 << 20),
        name="settle",
    )(*arrays)


def fused(rows, fine_assign, parent1, parent2, parent3, shrink):
    n = lax.axis_size("clus")
    m = lax.axis_size("dp")
    count, width = rows.shape
    fine_dev = parent1.shape[0]
    middle = parent2.shape[0]
    third = parent3.shape[0]
    share = width // n
    chunks = share // LANES
    pairs = m // 2
    half = LANES // 2
    thin = half // pairs
    fine = n * fine_dev
    total_rows = n * count
    vmem = pl.BlockSpec(memory_space=pltpu.VMEM)
    dma = pltpu.SemaphoreType.DMA
    fine_out, mid_out, coarse_out, spread = pl.pallas_call(
        functools.partial(sweep, n, m),
        out_shape=(
            jax.ShapeDtypeStruct((fine_dev, width), BF),
            jax.ShapeDtypeStruct((middle // n, width), BF),
            jax.ShapeDtypeStruct((third // (n * m), width), BF),
            jax.ShapeDtypeStruct((1, fine_dev), F32),
        ),
        in_specs=[vmem] * 4
        + [pl.BlockSpec(memory_space=pltpu.SMEM), pl.BlockSpec(memory_space=pltpu.HBM)],
        out_specs=[vmem] * 4,
        scratch_shapes=[
            pltpu.VMEM((n, 1, count), jnp.int32),
            pltpu.VMEM((n, 1, fine_dev), jnp.int32),
            pltpu.VMEM((total_rows, share), BF),
            pltpu.VMEM((fine, total_rows), BF),
            pltpu.VMEM((middle, total_rows), BF),
            pltpu.VMEM((third, total_rows), BF),
            pltpu.VMEM((total_rows, fine), BF),
            pltpu.VMEM((fine, middle), BF),
            pltpu.VMEM((third, middle), BF),
            pltpu.VMEM((fine, share), F32),
            pltpu.VMEM((middle, share), F32),
            pltpu.VMEM((fine, LANES), F32),
            pltpu.VMEM((middle, LANES), F32),
            pltpu.VMEM((chunks, LANES, third), F32),
            pltpu.VMEM((chunks, half, third), F32),
            pltpu.VMEM((chunks, half, third), F32),
            pltpu.VMEM((chunks, pairs, thin, third), F32),
            pltpu.VMEM((1, third), F32),
            pltpu.VMEM((m, 1, third), F32),
            pltpu.VMEM((chunks, LANES, third), BF),
            pltpu.VMEM((fine, share), BF),
            pltpu.VMEM((middle, share), BF),
            pltpu.VMEM((third, share), BF),
            pltpu.VMEM((n, 1, fine_dev), F32),
            pltpu.VMEM((n, 1, fine_dev), F32),
            pltpu.VMEM((n, 1, fine_dev), F32),
            dma((2, n)),
            dma((2, n)),
            dma((chunks, n)),
            dma((chunks, n)),
            dma((chunks,)),
            dma((chunks,)),
            dma((chunks, pairs)),
            dma((chunks, pairs)),
            dma((m,)),
            dma((m,)),
            dma((chunks, pairs)),
            dma((chunks, pairs)),
            dma((chunks,)),
            dma((chunks,)),
            dma((chunks, n)),
            dma((chunks, n)),
            dma((3, n)),
            dma((3, n)),
            dma((3 + chunks,)),
        ],
        compiler_params=pltpu.CompilerParams(
            collective_id=0, has_side_effects=True, vmem_limit_bytes=32 << 20
        ),
        name="sweep",
    )(
        fine_assign.reshape(1, count),
        parent1.reshape(1, fine_dev),
        parent2.reshape(1, middle),
        parent3.reshape(1, third),
        shrink,
        pltpu.with_memory_space_constraint(rows, pltpu.HBM),
    )
    fine_out, mid_out, coarse_out, spread = settle(fine_out, mid_out, coarse_out, spread)
    return fine_out, mid_out, coarse_out, spread.reshape(fine_dev)


def fits(rows, fine_assign, parent1, parent2, parent3):
    n = lax.axis_size("clus")
    m = lax.axis_size("dp")
    return (
        rows.shape[1] % (n * LANES) == 0
        and m % 2 == 0
        and (LANES // 2) % (m // 2 * 16) == 0
        and rows.shape[0] % LANES == 0
        and parent1.shape[0] % LANES == 0
        and parent2.shape[0] % LANES == 0
        and parent2.shape[0] <= 256
        and parent2.shape[0] % (n * 16) == 0
        and parent3.shape[0] % LANES == 0
        and parent3.shape[0] % (n * m * 16) == 0
    )


def step(rows, fine_assign, parent1, parent2, parent3, shrink):
    form = fused if fits(rows, fine_assign, parent1, parent2, parent3) else local
    return form(rows, fine_assign, parent1, parent2, parent3, shrink)


def solution(mesh):
    placed = (P(("dp", "clus"), None), P(("dp", "clus")), P(("dp", "clus")), P("dp"), P(), P())
    return jax.shard_map(
        step,
        mesh=mesh,
        in_specs=placed,
        out_specs=(
            P(("dp", "clus"), None),
            P(("dp", "clus"), None),
            P(("dp", "clus"), None),
            P(("dp", "clus")),
        ),
        check_vma=False,
    )
```
